512 devices in a mesh: light: 16 (over y, core), view: 32 (over z, x).
Axes of the slice: x: 4, y: 8, z: 8, core: 2. Of those that a mesh axis runs over, the one named last changes fastest.
Arguments:
- density: float32 [512, 128, 4096], P('light', 'view'), may hold values from 0.1 to 8
- emission: float32 [512, 128, 4096], P('light', 'view'), may hold values from 0.1 to 1
- facing: int32 [512], P('light'), may hold values 0 or 1
Outputs:
- radiance: float32 [512, 4096], P('light', 'view')
- coverage: float32 [512, 4096], P('light', 'view')
The draws below stay inside these ranges and needn't reach their ends.
All inputs are finite; a program needn't handle non-finite values. No bound on the sum of `facing` on one device may be relied on, other than what follows from the above.
Results may differ from the reference program's by a relative error of at most 0.0003.
Values sent between devices are 32-bit elements; how exact they have to be, the bound alone decides.
No kernel may reach another device: no remote copies, remote signals or barrier semaphores. Data moves between devices by JAX's collectives and lax.ppermute only.
A program may use at most 64 MiB of HBM per device.

```python
import math
import jax
import jax.numpy as jnp
from jax import lax

NP = 4096
NL = 512
NV = 128


def set_ends(array, key, smallest, top_value):
    extent = array.shape
    index_at = [jax.random.randint(jax.random.fold_in(key, axis), (), 0, extent[axis]) for axis in range(len(extent))]
    array = array.at[tuple(index_at)].set(smallest)
    longest = extent.index(max(extent))
    index_at[longest] = (index_at[longest] + 1) % extent[longest]
    return array.at[tuple(index_at)].set(top_value)


def levels(key, extent, split, least, top_value):
    level, own = 1.0, jax.random.fold_in(key, 6)
    for axis_at, parts in split:
        heights = jnp.exp(jax.random.uniform(jax.random.fold_in(own, axis_at), (parts,), jnp.float32, least / len(split), top_value / len(split)))
        level = level * jnp.repeat(heights, extent[axis_at] // parts).reshape([-1 if axis == axis_at else 1 for axis in range(len(extent))])
    return level


def setup_inputs(seed: int = 0) -> dict:
    splits = jax.random.split(jax.random.key(seed), 4)
    density = jnp.clip(jnp.exp(math.log(8.0) - 4.3820266 * jax.random.uniform(splits[0], (NL, NV, NP), jnp.float32) ** levels(splits[0], (NL, NV, NP), ((0, 16), (1, 32)), -0.2, 0.2)), 0.1, 8.0)
    emission = jnp.clip(0.1 + 0.9 * jax.random.uniform(splits[1], (NL, NV, NP), jnp.float32) ** levels(splits[1], (NL, NV, NP), ((0, 16), (1, 32)), -0.2, 0.2), 0.1, 1.0)
    facing = set_ends((jax.random.randint(splits[2], (NL,), 0, 2) < 1).astype(jnp.int32), jax.random.fold_in(splits[2], 1), 0, 1)
    return {"density": density, "emission": emission, "facing": facing}


def render_block(dens, emit, facing):
    nl = dens.shape[0]
    nv = dens.shape[1]
    tau_light = dens * (1.0 / nl)
    tau_view = dens * (1.0 / nv)
    depth = jnp.cumsum(tau_light, axis=0) - tau_light
    lit = emit * (0.2 + jnp.exp(-depth)) * (1.0 - jnp.exp(-tau_view))
    running = jnp.cumsum(tau_view, axis=1)
    before = running - tau_view
    total = jnp.sum(tau_view, axis=1)
    after = total[:, None, :] - running
    forward = jnp.sum(lit * jnp.exp(-before), axis=1)
    backward = jnp.sum(lit * jnp.exp(-after), axis=1)
    image = jnp.where((facing == 1)[:, None], backward, forward)
    return image, jnp.exp(-total)


def reference(density, emission, facing):
    nl, nv, npix = density.shape
    width = math.gcd(npix, 128)
    count = npix // width

    def one(index):
        start = (index * width).astype(jnp.int32)
        dens = lax.dynamic_slice_in_dim(density, start, width, 2)
        emit = lax.dynamic_slice_in_dim(emission, start, width, 2)
        return render_block(dens, emit, facing)

    images, covers = lax.map(one, jnp.arange(count, dtype=jnp.int32))
    radiance = jnp.moveaxis(images, 0, 1).reshape(nl, npix)
    coverage = jnp.moveaxis(covers, 0, 1).reshape(nl, npix)
    return radiance, coverage
```

```python
import jax
import jax.numpy as jnp
from jax import lax
from jax.sharding import PartitionSpec as P


def light_prefix(value):
    count = lax.axis_size("light")
    total = value
    received = jnp.zeros_like(value)
    shift = 1
    while shift < count:
        got = lax.ppermute(total, "light", [(i, i + shift) for i in range(count - shift)])
        total = total + got
        received = received + got
        shift *= 2
    return received


def group_exchange(block_of, my_pos, size, pairs_for):
    pieces = [block_of(my_pos)]
    for k in range(1, size):
        pieces.append(lax.ppermute(block_of((my_pos + k) % size), "view", pairs_for(k)))
    stacked = jnp.stack(pieces)
    return jnp.stack(
        [lax.dynamic_index_in_dim(stacked, (my_pos - j) % size, 0, keepdims=False) for j in range(size)]
    )


def composite(colors, transes, reversed_rows):
    count = colors.shape[0]
    forward = colors[count - 1]
    for j in range(count - 2, -1, -1):
        forward = colors[j] + transes[j] * forward
    backward = colors[0]
    for j in range(1, count):
        backward = colors[j] + transes[j] * backward
    return jnp.where(reversed_rows, backward, forward)


def make_shards(x_count):
    def shards(density, emission, facing):
        rows, cells, columns = density.shape
        light_count = lax.axis_size("light")
        view_count = lax.axis_size("view")
        z_count = view_count // x_count
        tau_light = density * (1.0 / (rows * light_count))
        tau_view = density * (1.0 / (cells * view_count))
        slab_depth = jnp.sum(tau_light, axis=0)
        incoming = light_prefix(slab_depth)

        reversed_rows = facing == 1
        local_depth = jnp.cumsum(tau_light, axis=0) - tau_light
        shade = jnp.exp(-local_depth)
        step = jnp.exp(-tau_view)
        forward_w = [jnp.ones_like(step[:, 0])]
        for v in range(1, cells):
            forward_w.append(forward_w[-1] * step[:, v - 1])
        backward_w = [jnp.ones_like(step[:, 0])]
        for v in range(cells - 2, -1, -1):
            backward_w.insert(0, backward_w[0] * step[:, v + 1])
        trans = forward_w[-1] * step[:, cells - 1]
        weight = jnp.where(reversed_rows[:, None, None], jnp.stack(backward_w, 1), jnp.stack(forward_w, 1))
        base = emission * (1.0 - step) * weight
        flat = jnp.sum(base, axis=1)
        lit_part = base * shade

        my_view = lax.axis_index("view")
        my_x = my_view % x_count
        my_z = my_view // x_count

        def pairs_x(k):
            return [(z * x_count + x, z * x_count + (x + k) % x_count) for z in range(z_count) for x in range(x_count)]

        def pairs_z(k):
            return [(z * x_count + x, ((z + k) % z_count) * x_count + x) for z in range(z_count) for x in range(x_count)]

        width = columns // view_count

        def x_blocks(array):
            grid = array.reshape(rows, z_count, x_count, width)
            return lambda pos: lax.dynamic_index_in_dim(grid, pos, 2, keepdims=False)

        def z_blocks(array):
            return lambda pos: lax.dynamic_index_in_dim(array, pos, 1, keepdims=False)

        trans_x = group_exchange(x_blocks(trans), my_x, x_count, pairs_x)
        trans_xg = jnp.prod(trans_x, axis=0)
        trans_z = group_exchange(z_blocks(trans_xg), my_z, z_count, pairs_z)
        coverage = jnp.prod(trans_z, axis=0)

        light = jnp.exp(-incoming)
        color = 0.2 * flat + jnp.sum(lit_part * light[None], axis=1)
        color_x = group_exchange(x_blocks(color), my_x, x_count, pairs_x)
        color_xg = composite(color_x, trans_x, reversed_rows[:, None, None])
        color_z = group_exchange(z_blocks(color_xg), my_z, z_count, pairs_z)
        radiance = composite(color_z, trans_z, reversed_rows[:, None])
        return (radiance, coverage)

    return shards


def x_extent(mesh):
    row = mesh.devices.reshape(mesh.devices.shape[0], -1)[0]
    coords = [getattr(d, "coords", None) for d in row]
    if any(c is None for c in coords):
        return 4
    first_z = coords[0][2]
    return sum(1 for c in coords if c[2] == first_z)


def solution(mesh):
    return jax.shard_map(
        make_shards(x_extent(mesh)),
        mesh=mesh,
        in_specs=(P("light", "view", None), P("light", "view", None), P("light")),
        out_specs=(P("light", "view"), P("light", "view")),
        check_vma=False,
    )
```

```python
import jax
import jax.numpy as jnp
from jax import lax
from jax.sharding import PartitionSpec as P


def light_prefix(value):
    count = lax.axis_size("light")
    cells, columns = value.shape
    chunks = value.reshape(cells, count, columns // count).transpose(1, 0, 2)
    mine = lax.all_to_all(chunks, "light", 0, 0)
    running = jnp.cumsum(mine, axis=0)
    before = jnp.concatenate([jnp.zeros_like(running[:1]), running[:-1]], axis=0)
    back = lax.all_to_all(before, "light", 0, 0)
    return back.transpose(1, 0, 2).reshape(cells, columns)


def group_exchange(block_of, my_pos, size, pairs_for):
    pieces = [block_of(my_pos)]
    for k in range(1, size):
        pieces.append(lax.ppermute(block_of((my_pos + k) % size), "view", pairs_for(k)))
    stacked = jnp.stack(pieces)
    return jnp.stack(
        [lax.dynamic_index_in_dim(stacked, (my_pos - j) % size, 0, keepdims=False) for j in range(size)]
    )


def composite(colors, transes, reversed_rows):
    count = colors.shape[0]
    forward = colors[count - 1]
    for j in range(count - 2, -1, -1):
        forward = colors[j] + transes[j] * forward
    backward = colors[0]
    for j in range(1, count):
        backward = colors[j] + transes[j] * backward
    return jnp.where(reversed_rows, backward, forward)


def make_shards(x_count):
    def shards(density, emission, facing):
        rows, cells, columns = density.shape
        light_count = lax.axis_size("light")
        view_count = lax.axis_size("view")
        z_count = view_count // x_count
        tau_light = density * (1.0 / (rows * light_count))
        tau_view = density * (1.0 / (cells * view_count))
        slab_depth = jnp.sum(tau_light, axis=0)
        incoming = light_prefix(slab_depth)

        reversed_rows = facing == 1
        local_depth = jnp.cumsum(tau_light, axis=0) - tau_light
        shade = jnp.exp(-local_depth)
        step = jnp.exp(-tau_view)
        forward_w = [jnp.ones_like(step[:, 0])]
        for v in range(1, cells):
            forward_w.append(forward_w[-1] * step[:, v - 1])
        backward_w = [jnp.ones_like(step[:, 0])]
        for v in range(cells - 2, -1, -1):
            backward_w.insert(0, backward_w[0] * step[:, v + 1])
        trans = forward_w[-1] * step[:, cells - 1]
        weight = jnp.where(reversed_rows[:, None, None], jnp.stack(backward_w, 1), jnp.stack(forward_w, 1))
        base = emission * (1.0 - step) * weight
        flat = jnp.sum(base, axis=1)
        lit_part = base * shade

        width = columns // view_count
        light = jnp.exp(-incoming)
        color = 0.2 * flat + jnp.sum(lit_part * light[None], axis=1)
        stacked = jnp.stack([color, trans]).reshape(2, rows, view_count, width).transpose(2, 0, 1, 3)
        pieces = lax.all_to_all(stacked, "view", 0, 0)
        radiance = composite(pieces[:, 0], pieces[:, 1], reversed_rows[:, None])
        coverage = jnp.prod(pieces[:, 1], axis=0)
        return (radiance, coverage)

    return shards


def x_extent(mesh):
    row = mesh.devices.reshape(mesh.devices.shape[0], -1)[0]
    coords = [getattr(d, "coords", None) for d in row]
    if any(c is None for c in coords):
        return 4
    first_z = coords[0][2]
    return sum(1 for c in coords if c[2] == first_z)


def solution(mesh):
    return jax.shard_map(
        make_shards(x_extent(mesh)),
        mesh=mesh,
        in_specs=(P("light", "view", None), P("light", "view", None), P("light")),
        out_specs=(P("light", "view"), P("light", "view")),
        check_vma=False,
    )
```

```python
import jax
import jax.numpy as jnp
from jax import lax
from jax.sharding import Mesh
from jax.sharding import PartitionSpec as P

VIEW = ("vz", "vx")


def light_prefix(value):
    count = lax.axis_size("light")
    cells, columns = value.shape
    chunks = value.reshape(cells, count, columns // count).transpose(1, 0, 2)
    mine = lax.all_to_all(chunks, "light", 0, 0)
    running = jnp.cumsum(mine, axis=0)
    before = jnp.concatenate([jnp.zeros_like(running[:1]), running[:-1]], axis=0)
    back = lax.all_to_all(before, "light", 0, 0)
    return back.transpose(1, 0, 2).reshape(cells, columns)


def composite(colors, transes, reversed_rows):
    count = colors.shape[0]
    forward = colors[count - 1]
    for j in range(count - 2, -1, -1):
        forward = colors[j] + transes[j] * forward
    backward = colors[0]
    for j in range(1, count):
        backward = colors[j] + transes[j] * backward
    return jnp.where(reversed_rows, backward, forward)


def shards(density, emission, facing):
    rows, cells, columns = density.shape
    light_count = lax.axis_size("light")
    z_count = lax.axis_size("vz")
    x_count = lax.axis_size("vx")
    view_count = z_count * x_count
    tau_light = density * (1.0 / (rows * light_count))
    tau_view = density * (1.0 / (cells * view_count))
    slab_depth = jnp.sum(tau_light, axis=0)
    incoming = light_prefix(slab_depth)

    reversed_rows = facing == 1
    local_depth = jnp.cumsum(tau_light, axis=0) - tau_light
    shade = jnp.exp(-local_depth)
    step = jnp.exp(-tau_view)
    forward_w = [jnp.ones_like(step[:, 0])]
    for v in range(1, cells):
        forward_w.append(forward_w[-1] * step[:, v - 1])
    backward_w = [jnp.ones_like(step[:, 0])]
    for v in range(cells - 2, -1, -1):
        backward_w.insert(0, backward_w[0] * step[:, v + 1])
    trans = forward_w[-1] * step[:, cells - 1]
    weight = jnp.where(reversed_rows[:, None, None], jnp.stack(backward_w, 1), jnp.stack(forward_w, 1))
    base = emission * (1.0 - step) * weight
    flat = jnp.sum(base, axis=1)
    lit_part = base * shade

    width = columns // view_count
    light = jnp.exp(-incoming)
    color = 0.2 * flat + jnp.sum(lit_part * light[None], axis=1)
    stacked = jnp.stack([color, trans]).reshape(2, rows, z_count, x_count, width).transpose(3, 0, 1, 2, 4)
    along_x = lax.all_to_all(stacked, "vx", 0, 0)
    color_x = composite(along_x[:, 0], along_x[:, 1], reversed_rows[:, None, None])
    trans_x = jnp.prod(along_x[:, 1], axis=0)
    stacked = jnp.stack([color_x, trans_x]).transpose(2, 0, 1, 3)
    along_z = lax.all_to_all(stacked, "vz", 0, 0)
    radiance = composite(along_z[:, 0], along_z[:, 1], reversed_rows[:, None])
    coverage = jnp.prod(along_z[:, 1], axis=0)
    return (radiance, coverage)


def view_split(mesh):
    row = mesh.devices.reshape(mesh.devices.shape[0], -1)[0]
    coords = [getattr(d, "coords", None) for d in row]
    if any(c is None for c in coords):
        return 1
    first_z = coords[0][2]
    return sum(1 for c in coords if c[2] == first_z)


def solution(mesh):
    x_count = view_split(mesh)
    light_count, view_count = mesh.devices.shape
    split = Mesh(mesh.devices.reshape(light_count, view_count // x_count, x_count), ("light",) + VIEW)
    return jax.shard_map(
        shards,
        mesh=split,
        in_specs=(P("light", VIEW, None), P("light", VIEW, None), P("light")),
        out_specs=(P("light", VIEW), P("light", VIEW)),
        check_vma=False,
    )
```

```python
import jax
import jax.numpy as jnp
from jax import lax
from jax.experimental import pallas as pl
from jax.experimental.pallas import tpu as pltpu
from jax.sharding import Mesh
from jax.sharding import PartitionSpec as P

VIEW = ("vz", "vx")


def light_prefix(value):
    count = lax.axis_size("light")
    cells, columns = value.shape
    chunks = value.reshape(cells, count, columns // count).transpose(1, 0, 2)
    mine = lax.all_to_all(chunks, "light", 0, 0)
    running = jnp.cumsum(mine, axis=0)
    before = jnp.concatenate([jnp.zeros_like(running[:1]), running[:-1]], axis=0)
    back = lax.all_to_all(before, "light", 0, 0)
    return back.transpose(1, 0, 2).reshape(cells, columns)


def shade_kernel(facing_ref, incoming_ref, dens_ref, emit_ref, color_ref, trans_ref, *, light_scale, view_scale):
    rows, cells, _ = dens_ref.shape

    def row(l, depth):
        dens = dens_ref[l]
        emit = emit_ref[l]
        tau_light = dens * light_scale
        step = jnp.exp(-(dens * view_scale))
        lit = emit * (0.2 + jnp.exp(-depth)) * (1.0 - step)
        s = [step[v:v + 1] for v in range(cells)]
        c = [lit[v:v + 1] for v in range(cells)]
        forward = c[cells - 1]
        for v in range(cells - 2, -1, -1):
            forward = c[v] + s[v] * forward
        backward = c[0]
        for v in range(1, cells):
            backward = c[v] + s[v] * backward
        trans = s[0]
        for v in range(1, cells):
            trans = trans * s[v]
        color_ref[pl.ds(l, 1), :] = jnp.where(facing_ref[l] == 1, backward, forward)
        trans_ref[pl.ds(l, 1), :] = trans
        return depth + tau_light

    lax.fori_loop(0, rows, row, incoming_ref[...], unroll=8)


def shade(facing, incoming, density, emission, light_scale, view_scale, tile=512):
    rows, cells, columns = density.shape
    tile = min(tile, columns)
    body = lambda *refs: shade_kernel(*refs, light_scale=light_scale, view_scale=view_scale)
    return pl.pallas_call(
        body,
        grid=(columns // tile,),
        in_specs=[
            pl.BlockSpec(memory_space=pltpu.SMEM),
            pl.BlockSpec((cells, tile), lambda j: (0, j)),
            pl.BlockSpec((rows, cells, tile), lambda j: (0, 0, j)),
            pl.BlockSpec((rows, cells, tile), lambda j: (0, 0, j)),
        ],
        out_specs=[
            pl.BlockSpec((rows, tile), lambda j: (0, j)),
            pl.BlockSpec((rows, tile), lambda j: (0, j)),
        ],
        out_shape=[jax.ShapeDtypeStruct((rows, columns), jnp.float32)] * 2,
        cost_estimate=pl.CostEstimate(
            flops=30 * density.size, transcendentals=2 * density.size, bytes_accessed=2 * 4 * density.size + 8 * rows * columns
        ),
    )(facing, incoming, density, emission)


def composite(colors, transes, reversed_rows):
    count = colors.shape[0]
    forward = colors[count - 1]
    for j in range(count - 2, -1, -1):
        forward = colors[j] + transes[j] * forward
    backward = colors[0]
    for j in range(1, count):
        backward = colors[j] + transes[j] * backward
    return jnp.where(reversed_rows, backward, forward)


def shards(density, emission, facing):
    rows, cells, columns = density.shape
    light_count = lax.axis_size("light")
    z_count = lax.axis_size("vz")
    x_count = lax.axis_size("vx")
    view_count = z_count * x_count
    tau_light = density * (1.0 / (rows * light_count))
    slab_depth = jnp.sum(tau_light, axis=0)
    incoming = light_prefix(slab_depth)

    reversed_rows = facing == 1
    width = columns // view_count
    color, trans = shade(facing, incoming, density, emission, 1.0 / (rows * light_count), 1.0 / (cells * view_count))
    stacked = jnp.stack([color, trans]).reshape(2, rows, z_count, x_count, width).transpose(3, 0, 1, 2, 4)
    along_x = lax.all_to_all(stacked, "vx", 0, 0)
    color_x = composite(along_x[:, 0], along_x[:, 1], reversed_rows[:, None, None])
    trans_x = jnp.prod(along_x[:, 1], axis=0)
    stacked = jnp.stack([color_x, trans_x]).transpose(2, 0, 1, 3)
    along_z = lax.all_to_all(stacked, "vz", 0, 0)
    radiance = composite(along_z[:, 0], along_z[:, 1], reversed_rows[:, None])
    coverage = jnp.prod(along_z[:, 1], axis=0)
    return (radiance, coverage)


def view_split(mesh):
    row = mesh.devices.reshape(mesh.devices.shape[0], -1)[0]
    coords = [getattr(d, "coords", None) for d in row]
    if any(c is None for c in coords):
        return 1
    first_z = coords[0][2]
    return sum(1 for c in coords if c[2] == first_z)


def solution(mesh):
    x_count = view_split(mesh)
    light_count, view_count = mesh.devices.shape
    split = Mesh(mesh.devices.reshape(light_count, view_count // x_count, x_count), ("light",) + VIEW)
    return jax.shard_map(
        shards,
        mesh=split,
        in_specs=(P("light", VIEW, None), P("light", VIEW, None), P("light")),
        out_specs=(P("light", VIEW), P("light", VIEW)),
        check_vma=False,
    )
```

```python
import jax
import jax.numpy as jnp
from jax import lax
from jax.experimental import pallas as pl
from jax.experimental.pallas import tpu as pltpu
from jax.sharding import Mesh
from jax.sharding import PartitionSpec as P

VIEW = ("vz", "vx")


def light_prefix(value):
    count = lax.axis_size("light")
    cells, columns = value.shape
    chunks = value.reshape(cells, count, columns // count).transpose(1, 0, 2)
    mine = lax.all_to_all(chunks, "light", 0, 0)
    running = jnp.cumsum(mine, axis=0)
    before = jnp.concatenate([jnp.zeros_like(running[:1]), running[:-1]], axis=0)
    back = lax.all_to_all(before, "light", 0, 0)
    return back.transpose(1, 0, 2).reshape(cells, columns)


def shade_kernel(facing_ref, incoming_ref, dens_ref, emit_ref, out_ref, *, light_scale, view_scale):
    rows, cells, _ = dens_ref.shape
    blocks, width = out_ref.shape[0], out_ref.shape[-1]

    def row(l, depth):
        dens = dens_ref[l]
        emit = emit_ref[l]
        tau_light = dens * light_scale
        step = jnp.exp(-(dens * view_scale))
        lit = emit * (0.2 + jnp.exp(-depth)) * (1.0 - step)
        s = [step[v:v + 1] for v in range(cells)]
        c = [lit[v:v + 1] for v in range(cells)]
        forward = c[cells - 1]
        for v in range(cells - 2, -1, -1):
            forward = c[v] + s[v] * forward
        backward = c[0]
        for v in range(1, cells):
            backward = c[v] + s[v] * backward
        trans = s[0]
        for v in range(1, cells):
            trans = trans * s[v]
        color = jnp.where(facing_ref[l] == 1, backward, forward)
        for b in range(blocks):
            out_ref[b, 0, 0, pl.ds(l, 1), :] = color[:, b * width:(b + 1) * width]
            out_ref[b, 1, 0, pl.ds(l, 1), :] = trans[:, b * width:(b + 1) * width]
        return depth + tau_light

    lax.fori_loop(0, rows, row, incoming_ref[...], unroll=8)


def shade(facing, incoming, density, emission, light_scale, view_scale, blocks, width):
    rows, cells, columns = density.shape
    tile = blocks * width
    tiles = columns // tile
    body = lambda *refs: shade_kernel(*refs, light_scale=light_scale, view_scale=view_scale)
    return pl.pallas_call(
        body,
        grid=(tiles,),
        in_specs=[
            pl.BlockSpec(memory_space=pltpu.SMEM),
            pl.BlockSpec((cells, tile), lambda j: (0, j)),
            pl.BlockSpec((rows, cells, tile), lambda j: (0, 0, j)),
            pl.BlockSpec((rows, cells, tile), lambda j: (0, 0, j)),
        ],
        out_specs=pl.BlockSpec((blocks, 2, 1, rows, width), lambda j: (0, 0, j, 0, 0)),
        out_shape=jax.ShapeDtypeStruct((blocks, 2, tiles, rows, width), jnp.float32),
        cost_estimate=pl.CostEstimate(
            flops=30 * density.size, transcendentals=2 * density.size, bytes_accessed=2 * 4 * density.size + 8 * rows * columns
        ),
    )(facing, incoming, density, emission)


def composite(colors, transes, reversed_rows):
    count = colors.shape[0]
    forward = colors[count - 1]
    for j in range(count - 2, -1, -1):
        forward = colors[j] + transes[j] * forward
    backward = colors[0]
    for j in range(1, count):
        backward = colors[j] + transes[j] * backward
    return jnp.where(reversed_rows, backward, forward)


def shards(density, emission, facing):
    rows, cells, columns = density.shape
    light_count = lax.axis_size("light")
    z_count = lax.axis_size("vz")
    x_count = lax.axis_size("vx")
    view_count = z_count * x_count
    tau_light = density * (1.0 / (rows * light_count))
    slab_depth = jnp.sum(tau_light, axis=0)
    incoming = light_prefix(slab_depth)

    reversed_rows = facing == 1
    width = columns // view_count
    stacked = shade(
        facing, incoming, density, emission, 1.0 / (rows * light_count), 1.0 / (cells * view_count), x_count, width
    )
    along_x = lax.all_to_all(stacked, "vx", 0, 0)
    color_x = composite(along_x[:, 0], along_x[:, 1], reversed_rows[None, :, None])
    trans_x = jnp.prod(along_x[:, 1], axis=0)
    along_z = lax.all_to_all(jnp.stack([color_x, trans_x], axis=1), "vz", 0, 0)
    radiance = composite(along_z[:, 0], along_z[:, 1], reversed_rows[:, None])
    coverage = jnp.prod(along_z[:, 1], axis=0)
    return (radiance, coverage)


def view_split(mesh):
    row = mesh.devices.reshape(mesh.devices.shape[0], -1)[0]
    coords = [getattr(d, "coords", None) for d in row]
    if any(c is None for c in coords):
        return 1
    first_z = coords[0][2]
    return sum(1 for c in coords if c[2] == first_z)


def solution(mesh):
    x_count = view_split(mesh)
    light_count, view_count = mesh.devices.shape
    split = Mesh(mesh.devices.reshape(light_count, view_count // x_count, x_count), ("light",) + VIEW)
    return jax.shard_map(
        shards,
        mesh=split,
        in_specs=(P("light", VIEW, None), P("light", VIEW, None), P("light")),
        out_specs=(P("light", VIEW), P("light", VIEW)),
        check_vma=False,
    )
```

```python
import jax
import jax.numpy as jnp
from jax import lax
from jax.experimental import pallas as pl
from jax.experimental.pallas import tpu as pltpu
from jax.sharding import Mesh
from jax.sharding import PartitionSpec as P

VIEW = ("vz", "vx")


def light_prefix(value):
    count = lax.axis_size("light")
    cells, columns = value.shape
    chunks = value.reshape(cells, count, columns // count).transpose(1, 0, 2)
    mine = lax.all_to_all(chunks, "light", 0, 0)
    running = jnp.cumsum(mine, axis=0)
    before = jnp.concatenate([jnp.zeros_like(running[:1]), running[:-1]], axis=0)
    back = lax.all_to_all(before, "light", 0, 0)
    return back.transpose(1, 0, 2).reshape(cells, columns)


def shade_kernel(facing_ref, incoming_ref, dens_ref, emit_ref, out_ref, *, light_scale, view_scale):
    rows, cells, _ = dens_ref.shape
    blocks, width = out_ref.shape[0], out_ref.shape[-1]

    def row(l, depth):
        dens = dens_ref[l]
        emit = emit_ref[l]
        tau_light = dens * light_scale
        step = jnp.exp(-(dens * view_scale))
        lit = emit * (0.2 + jnp.exp(-depth)) * (1.0 - step)
        s = [step[v:v + 1] for v in range(cells)]
        c = [lit[v:v + 1] for v in range(cells)]
        forward = c[cells - 1]
        for v in range(cells - 2, -1, -1):
            forward = c[v] + s[v] * forward
        backward = c[0]
        for v in range(1, cells):
            backward = c[v] + s[v] * backward
        color = jnp.where(facing_ref[l] == 1, backward, forward)
        for b in range(blocks):
            out_ref[b, 0, pl.ds(l, 1), :] = color[:, b * width:(b + 1) * width]
        return depth + tau_light

    lax.fori_loop(0, rows, row, incoming_ref[...], unroll=8)


def shade(facing, incoming, density, emission, light_scale, view_scale, blocks, width):
    rows, cells, columns = density.shape
    tile = blocks * width
    tiles = columns // tile
    body = lambda *refs: shade_kernel(*refs, light_scale=light_scale, view_scale=view_scale)
    return pl.pallas_call(
        body,
        grid=(tiles,),
        in_specs=[
            pl.BlockSpec(memory_space=pltpu.SMEM),
            pl.BlockSpec((cells, tile), lambda j: (0, j)),
            pl.BlockSpec((rows, cells, tile), lambda j: (0, 0, j)),
            pl.BlockSpec((rows, cells, tile), lambda j: (0, 0, j)),
        ],
        out_specs=pl.BlockSpec((blocks, 1, rows, width), lambda j: (0, j, 0, 0)),
        out_shape=jax.ShapeDtypeStruct((blocks, tiles, rows, width), jnp.float32),
        cost_estimate=pl.CostEstimate(
            flops=30 * density.size, transcendentals=2 * density.size, bytes_accessed=2 * 4 * density.size + 8 * rows * columns
        ),
    )(facing, incoming, density, emission)


def composite(colors, transes, reversed_rows):
    count = colors.shape[0]
    forward = colors[count - 1]
    for j in range(count - 2, -1, -1):
        forward = colors[j] + transes[j] * forward
    backward = colors[0]
    for j in range(1, count):
        backward = colors[j] + transes[j] * backward
    return jnp.where(reversed_rows, backward, forward)


def shards(density, emission, facing):
    rows, cells, columns = density.shape
    light_count = lax.axis_size("light")
    z_count = lax.axis_size("vz")
    x_count = lax.axis_size("vx")
    view_count = z_count * x_count
    tau_light = density * (1.0 / (rows * light_count))
    slab_depth = jnp.sum(tau_light, axis=0)
    width = columns // view_count
    trans = jnp.exp(-jnp.sum(density * (1.0 / (cells * view_count)), axis=1))
    trans_blocks = trans.reshape(rows, z_count, x_count, width).transpose(2, 1, 0, 3)
    trans_x = lax.all_to_all(trans_blocks, "vx", 0, 0)
    incoming = light_prefix(slab_depth)

    reversed_rows = facing == 1
    color = shade(
        facing, incoming, density, emission, 1.0 / (rows * light_count), 1.0 / (cells * view_count), x_count, width
    )
    color_x = lax.all_to_all(color, "vx", 0, 0)
    color_xg = composite(color_x, trans_x, reversed_rows[None, :, None])
    trans_xg = jnp.prod(trans_x, axis=0)
    along_z = lax.all_to_all(jnp.stack([color_xg, trans_xg], axis=1), "vz", 0, 0)
    radiance = composite(along_z[:, 0], along_z[:, 1], reversed_rows[:, None])
    coverage = jnp.prod(along_z[:, 1], axis=0)
    return (radiance, coverage)


def view_split(mesh):
    row = mesh.devices.reshape(mesh.devices.shape[0], -1)[0]
    coords = [getattr(d, "coords", None) for d in row]
    if any(c is None for c in coords):
        return 1
    first_z = coords[0][2]
    return sum(1 for c in coords if c[2] == first_z)


def solution(mesh):
    x_count = view_split(mesh)
    light_count, view_count = mesh.devices.shape
    split = Mesh(mesh.devices.reshape(light_count, view_count // x_count, x_count), ("light",) + VIEW)
    return jax.shard_map(
        shards,
        mesh=split,
        in_specs=(P("light", VIEW, None), P("light", VIEW, None), P("light")),
        out_specs=(P("light", VIEW), P("light", VIEW)),
        check_vma=False,
    )
```

```python
import jax
import jax.numpy as jnp
from jax import lax
from jax.experimental import pallas as pl
from jax.experimental.pallas import tpu as pltpu
from jax.sharding import Mesh
from jax.sharding import PartitionSpec as P

VIEW = ("vz", "vx")


def light_prefix(value):
    count = lax.axis_size("light")
    cells, columns = value.shape
    chunks = value.reshape(cells, count, columns // count).transpose(1, 0, 2)
    mine = lax.all_to_all(chunks, "light", 0, 0)
    running = jnp.cumsum(mine, axis=0)
    before = jnp.concatenate([jnp.zeros_like(running[:1]), running[:-1]], axis=0)
    back = lax.all_to_all(before, "light", 0, 0)
    return back.transpose(1, 0, 2).reshape(cells, columns)


def shade_kernel(facing_ref, incoming_ref, dens_ref, emit_ref, out_ref, *, light_scale, view_scale):
    rows, cells, _ = dens_ref.shape
    blocks, width = out_ref.shape[0], out_ref.shape[-1]

    def row(l, depth):
        dens = dens_ref[l]
        emit = emit_ref[l]
        tau_light = dens * light_scale
        step = jnp.exp(-(dens * view_scale))
        lit = emit * (0.2 + jnp.exp(-depth)) * (1.0 - step)
        s = [step[v:v + 1] for v in range(cells)]
        c = [lit[v:v + 1] for v in range(cells)]
        forward = c[cells - 1]
        for v in range(cells - 2, -1, -1):
            forward = c[v] + s[v] * forward
        backward = c[0]
        for v in range(1, cells):
            backward = c[v] + s[v] * backward
        trans = s[0]
        for v in range(1, cells):
            trans = trans * s[v]
        color = jnp.where(facing_ref[l] == 1, backward, forward)
        for b in range(blocks):
            out_ref[b, 0, 0, pl.ds(l, 1), :] = color[:, b * width:(b + 1) * width]
            out_ref[b, 1, 0, pl.ds(l, 1), :] = trans[:, b * width:(b + 1) * width]
        return depth + tau_light

    lax.fori_loop(0, rows, row, incoming_ref[...], unroll=8)


def shade(facing, incoming, density, emission, light_scale, view_scale, blocks, width):
    rows, cells, columns = density.shape
    tile = blocks * width
    tiles = columns // tile
    body = lambda *refs: shade_kernel(*refs, light_scale=light_scale, view_scale=view_scale)
    return pl.pallas_call(
        body,
        grid=(tiles,),
        in_specs=[
            pl.BlockSpec(memory_space=pltpu.SMEM),
            pl.BlockSpec((cells, tile), lambda j: (0, j)),
            pl.BlockSpec((rows, cells, tile), lambda j: (0, 0, j)),
            pl.BlockSpec((rows, cells, tile), lambda j: (0, 0, j)),
        ],
        out_specs=pl.BlockSpec((blocks, 2, 1, rows, width), lambda j: (0, 0, j, 0, 0)),
        out_shape=jax.ShapeDtypeStruct((blocks, 2, tiles, rows, width), jnp.float32),
        cost_estimate=pl.CostEstimate(
            flops=30 * density.size, transcendentals=2 * density.size, bytes_accessed=2 * 4 * density.size + 8 * rows * columns
        ),
    )(facing, incoming, density, emission)


def composite(colors, transes, reversed_rows):
    count = colors.shape[0]
    forward = colors[count - 1]
    for j in range(count - 2, -1, -1):
        forward = colors[j] + transes[j] * forward
    backward = colors[0]
    for j in range(1, count):
        backward = colors[j] + transes[j] * backward
    return jnp.where(reversed_rows, backward, forward)


def halving(stacked, axis, reversed_rows):
    count = lax.axis_size(axis)
    mine = lax.axis_index(axis)
    bit = 0
    while (1 << bit) < count:
        _, blocks, rows, width = stacked.shape
        paired = stacked.reshape(2, blocks // 2, 2, rows, width)
        my_bit = mine >> bit & 1
        keep = jnp.where(my_bit == 1, paired[:, :, 1], paired[:, :, 0])
        send = jnp.where(my_bit == 1, paired[:, :, 0], paired[:, :, 1])
        got = lax.ppermute(send, axis, [(i, i ^ (1 << bit)) for i in range(count)])
        in_front = ((my_bit == 0) == jnp.logical_not(reversed_rows))[None, :, None]
        front = jnp.where(in_front, keep, got)
        back = jnp.where(in_front, got, keep)
        stacked = jnp.stack([front[0] + front[1] * back[0], front[1] * back[1]])
        bit += 1
    return stacked[0, 0], stacked[1, 0]


def shards(density, emission, facing):
    rows, cells, columns = density.shape
    light_count = lax.axis_size("light")
    z_count = lax.axis_size("vz")
    x_count = lax.axis_size("vx")
    view_count = z_count * x_count
    tau_light = density * (1.0 / (rows * light_count))
    slab_depth = jnp.sum(tau_light, axis=0)
    incoming = light_prefix(slab_depth)

    reversed_rows = facing == 1
    width = columns // view_count
    stacked = shade(
        facing, incoming, density, emission, 1.0 / (rows * light_count), 1.0 / (cells * view_count), x_count, width
    )
    along_x = lax.all_to_all(stacked, "vx", 0, 0)
    color_x = composite(along_x[:, 0], along_x[:, 1], reversed_rows[None, :, None])
    trans_x = jnp.prod(along_x[:, 1], axis=0)
    radiance, coverage = halving(jnp.stack([color_x, trans_x]), "vz", reversed_rows)
    return (radiance, coverage)


def view_split(mesh):
    row = mesh.devices.reshape(mesh.devices.shape[0], -1)[0]
    coords = [getattr(d, "coords", None) for d in row]
    if any(c is None for c in coords):
        return 1
    first_z = coords[0][2]
    return sum(1 for c in coords if c[2] == first_z)


def solution(mesh):
    x_count = view_split(mesh)
    light_count, view_count = mesh.devices.shape
    split = Mesh(mesh.devices.reshape(light_count, view_count // x_count, x_count), ("light",) + VIEW)
    return jax.shard_map(
        shards,
        mesh=split,
        in_specs=(P("light", VIEW, None), P("light", VIEW, None), P("light")),
        out_specs=(P("light", VIEW), P("light", VIEW)),
        check_vma=False,
    )
```

```python
import jax
import jax.numpy as jnp
from jax import lax
from jax.experimental import pallas as pl
from jax.experimental.pallas import tpu as pltpu
from jax.sharding import Mesh
from jax.sharding import PartitionSpec as P

VIEW = ("vz", "vx")


def light_prefix(value):
    count = lax.axis_size("light")
    cells, columns = value.shape
    chunks = value.reshape(cells, count, columns // count).transpose(1, 0, 2)
    mine = lax.all_to_all(chunks, "light", 0, 0)
    running = jnp.cumsum(mine, axis=0)
    before = jnp.concatenate([jnp.zeros_like(running[:1]), running[:-1]], axis=0)
    back = lax.all_to_all(before, "light", 0, 0)
    return back.transpose(1, 0, 2).reshape(cells, columns)


def shade_kernel(facing_ref, dens_ref, emit_ref, out_ref, part_ref, *, light_scale, view_scale):
    rows, cells, _ = dens_ref.shape
    blocks, width = out_ref.shape[0], out_ref.shape[-1]

    def row(l, depth):
        dens = dens_ref[l]
        emit = emit_ref[l]
        tau_light = dens * light_scale
        step = jnp.exp(-(dens * view_scale))
        base = emit * (1.0 - step)
        shaded = base * jnp.exp(-depth)
        s = [step[v:v + 1] for v in range(cells)]
        flip = facing_ref[l] == 1
        ahead = [None] * cells
        behind = [None] * cells
        ahead[0] = jnp.ones_like(s[0])
        for v in range(1, cells):
            ahead[v] = ahead[v - 1] * s[v - 1]
        behind[cells - 1] = jnp.ones_like(s[0])
        for v in range(cells - 2, -1, -1):
            behind[v] = behind[v + 1] * s[v + 1]
        weight = [jnp.where(flip, behind[v], ahead[v]) for v in range(cells)]
        flat = weight[0] * base[0:1]
        for v in range(1, cells):
            flat = flat + weight[v] * base[v:v + 1]
        trans = ahead[cells - 1] * s[cells - 1]
        for b in range(blocks):
            cut = slice(b * width, (b + 1) * width)
            out_ref[b, 0, 0, pl.ds(l, 1), :] = 0.2 * flat[:, cut]
            out_ref[b, 1, 0, pl.ds(l, 1), :] = trans[:, cut]
            for v in range(cells):
                part_ref[v, b, 0, pl.ds(l, 1), :] = (weight[v] * shaded[v:v + 1])[:, cut]
        return depth + tau_light

    lax.fori_loop(0, rows, row, jnp.zeros(dens_ref.shape[1:], jnp.float32), unroll=8)


def shade(facing, density, emission, light_scale, view_scale, blocks, width):
    rows, cells, columns = density.shape
    tile = blocks * width
    tiles = columns // tile
    body = lambda *refs: shade_kernel(*refs, light_scale=light_scale, view_scale=view_scale)
    return pl.pallas_call(
        body,
        grid=(tiles,),
        in_specs=[
            pl.BlockSpec(memory_space=pltpu.SMEM),
            pl.BlockSpec((rows, cells, tile), lambda j: (0, 0, j)),
            pl.BlockSpec((rows, cells, tile), lambda j: (0, 0, j)),
        ],
        out_specs=[
            pl.BlockSpec((blocks, 2, 1, rows, width), lambda j: (0, 0, j, 0, 0)),
            pl.BlockSpec((cells, blocks, 1, rows, width), lambda j: (0, 0, j, 0, 0)),
        ],
        out_shape=[
            jax.ShapeDtypeStruct((blocks, 2, tiles, rows, width), jnp.float32),
            jax.ShapeDtypeStruct((cells, blocks, tiles, rows, width), jnp.float32),
        ],
        cost_estimate=pl.CostEstimate(
            flops=40 * density.size, transcendentals=2 * density.size, bytes_accessed=4 * 4 * density.size + 8 * rows * columns
        ),
    )(facing, density, emission)


def composite(colors, transes, reversed_rows):
    count = colors.shape[0]
    forward = colors[count - 1]
    for j in range(count - 2, -1, -1):
        forward = colors[j] + transes[j] * forward
    backward = colors[0]
    for j in range(1, count):
        backward = colors[j] + transes[j] * backward
    return jnp.where(reversed_rows, backward, forward)


def shards(density, emission, facing):
    rows, cells, columns = density.shape
    light_count = lax.axis_size("light")
    z_count = lax.axis_size("vz")
    x_count = lax.axis_size("vx")
    view_count = z_count * x_count
    tau_light = density * (1.0 / (rows * light_count))
    slab_depth = jnp.sum(tau_light, axis=0)
    reversed_rows = facing == 1
    width = columns // view_count
    unshaded, parts = shade(
        facing, density, emission, 1.0 / (rows * light_count), 1.0 / (cells * view_count), x_count, width
    )
    incoming = light_prefix(slab_depth)
    light = jnp.exp(-incoming).reshape(cells, z_count, x_count, 1, width).transpose(0, 2, 1, 3, 4)
    color = unshaded[:, 0] + jnp.sum(light * parts, axis=0)
    stacked = jnp.stack([color, unshaded[:, 1]], axis=1)
    along_x = lax.all_to_all(stacked, "vx", 0, 0)
    color_x = composite(along_x[:, 0], along_x[:, 1], reversed_rows[None, :, None])
    trans_x = jnp.prod(along_x[:, 1], axis=0)
    along_z = lax.all_to_all(jnp.stack([color_x, trans_x], axis=1), "vz", 0, 0)
    radiance = composite(along_z[:, 0], along_z[:, 1], reversed_rows[:, None])
    coverage = jnp.prod(along_z[:, 1], axis=0)
    return (radiance, coverage)


def view_split(mesh):
    row = mesh.devices.reshape(mesh.devices.shape[0], -1)[0]
    coords = [getattr(d, "coords", None) for d in row]
    if any(c is None for c in coords):
        return 1
    first_z = coords[0][2]
    return sum(1 for c in coords if c[2] == first_z)


def solution(mesh):
    x_count = view_split(mesh)
    light_count, view_count = mesh.devices.shape
    split = Mesh(mesh.devices.reshape(light_count, view_count // x_count, x_count), ("light",) + VIEW)
    return jax.shard_map(
        shards,
        mesh=split,
        in_specs=(P("light", VIEW, None), P("light", VIEW, None), P("light")),
        out_specs=(P("light", VIEW), P("light", VIEW)),
        check_vma=False,
    )
```

```python
import jax
import jax.numpy as jnp
from jax import lax
from jax.experimental import pallas as pl
from jax.experimental.pallas import tpu as pltpu
from jax.sharding import Mesh
from jax.sharding import PartitionSpec as P

VIEW = ("vz", "vx")


def light_prefix(value):
    count = lax.axis_size("light")
    cells, columns = value.shape
    chunks = value.reshape(cells, count, columns // count).transpose(1, 0, 2)
    mine = lax.all_to_all(chunks, "light", 0, 0)
    running = jnp.cumsum(mine, axis=0)
    before = jnp.concatenate([jnp.zeros_like(running[:1]), running[:-1]], axis=0)
    back = lax.all_to_all(before, "light", 0, 0)
    return back.transpose(1, 0, 2).reshape(cells, columns)


def shade_kernel(facing_ref, dens_ref, emit_ref, out_ref, part_ref, *, light_scale, view_scale):
    rows, cells, _ = dens_ref.shape
    blocks, width = out_ref.shape[0], out_ref.shape[-1]

    def row(l, depth):
        dens = dens_ref[l]
        emit = emit_ref[l]
        tau_light = dens * light_scale
        step = jnp.exp(-(dens * view_scale))
        base = emit * (1.0 - step)
        shaded = base * jnp.exp(-depth)
        s = [step[v:v + 1] for v in range(cells)]
        flip = facing_ref[l] == 1
        ahead = [None] * cells
        behind = [None] * cells
        ahead[0] = jnp.ones_like(s[0])
        for v in range(1, cells):
            ahead[v] = ahead[v - 1] * s[v - 1]
        behind[cells - 1] = jnp.ones_like(s[0])
        for v in range(cells - 2, -1, -1):
            behind[v] = behind[v + 1] * s[v + 1]
        weight = [jnp.where(flip, behind[v], ahead[v]) for v in range(cells)]
        flat = weight[0] * base[0:1]
        for v in range(1, cells):
            flat = flat + weight[v] * base[v:v + 1]
        trans = ahead[cells - 1] * s[cells - 1]
        for b in range(blocks):
            cut = slice(b * width, (b + 1) * width)
            out_ref[b, 0, 0, pl.ds(l, 1), :] = 0.2 * flat[:, cut]
            out_ref[b, 1, 0, pl.ds(l, 1), :] = trans[:, cut]
            for v in range(cells):
                part_ref[v, b, 0, pl.ds(l, 1), :] = (weight[v] * shaded[v:v + 1])[:, cut]
        return depth + tau_light

    lax.fori_loop(0, rows, row, jnp.zeros(dens_ref.shape[1:], jnp.float32), unroll=8)


def shade(facing, density, emission, light_scale, view_scale, blocks, width):
    rows, cells, columns = density.shape
    tile = blocks * width
    tiles = columns // tile
    body = lambda *refs: shade_kernel(*refs, light_scale=light_scale, view_scale=view_scale)
    return pl.pallas_call(
        body,
        grid=(tiles,),
        in_specs=[
            pl.BlockSpec(memory_space=pltpu.SMEM),
            pl.BlockSpec((rows, cells, tile), lambda j: (0, 0, j)),
            pl.BlockSpec((rows, cells, tile), lambda j: (0, 0, j)),
        ],
        out_specs=[
            pl.BlockSpec((blocks, 2, 1, rows, width), lambda j: (0, 0, j, 0, 0)),
            pl.BlockSpec((cells, blocks, 1, rows, width), lambda j: (0, 0, j, 0, 0)),
        ],
        out_shape=[
            jax.ShapeDtypeStruct((blocks, 2, tiles, rows, width), jnp.float32),
            jax.ShapeDtypeStruct((cells, blocks, tiles, rows, width), jnp.float32),
        ],
        cost_estimate=pl.CostEstimate(
            flops=40 * density.size, transcendentals=2 * density.size, bytes_accessed=4 * 4 * density.size + 8 * rows * columns
        ),
    )(facing, density, emission)


def composite(colors, transes, reversed_rows):
    count = colors.shape[0]
    forward = colors[count - 1]
    for j in range(count - 2, -1, -1):
        forward = colors[j] + transes[j] * forward
    backward = colors[0]
    for j in range(1, count):
        backward = colors[j] + transes[j] * backward
    return jnp.where(reversed_rows, backward, forward)


def shards(density, emission, facing):
    rows, cells, columns = density.shape
    light_count = lax.axis_size("light")
    z_count = lax.axis_size("vz")
    x_count = lax.axis_size("vx")
    view_count = z_count * x_count
    tau_light = density * (1.0 / (rows * light_count))
    slab_depth = jnp.sum(tau_light, axis=0)
    reversed_rows = facing == 1
    width = columns // view_count
    unshaded, parts = shade(
        facing, density, emission, 1.0 / (rows * light_count), 1.0 / (cells * view_count), x_count, width
    )
    incoming = light_prefix(slab_depth)
    light = jnp.exp(-incoming).reshape(cells, z_count, x_count, 1, width).transpose(0, 2, 1, 3, 4)
    stacked = unshaded.at[:, 0].add(jnp.sum(light * parts, axis=0))
    along_x = lax.all_to_all(stacked, "vx", 0, 0)
    color_x = composite(along_x[:, 0], along_x[:, 1], reversed_rows[None, :, None])
    trans_x = jnp.prod(along_x[:, 1], axis=0)
    along_z = lax.all_to_all(jnp.stack([color_x, trans_x], axis=1), "vz", 0, 0)
    radiance = composite(along_z[:, 0], along_z[:, 1], reversed_rows[:, None])
    coverage = jnp.prod(along_z[:, 1], axis=0)
    return (radiance, coverage)


def view_split(mesh):
    row = mesh.devices.reshape(mesh.devices.shape[0], -1)[0]
    coords = [getattr(d, "coords", None) for d in row]
    if any(c is None for c in coords):
        return 1
    first_z = coords[0][2]
    return sum(1 for c in coords if c[2] == first_z)


def solution(mesh):
    x_count = view_split(mesh)
    light_count, view_count = mesh.devices.shape
    split = Mesh(mesh.devices.reshape(light_count, view_count // x_count, x_count), ("light",) + VIEW)
    return jax.shard_map(
        shards,
        mesh=split,
        in_specs=(P("light", VIEW, None), P("light", VIEW, None), P("light")),
        out_specs=(P("light", VIEW), P("light", VIEW)),
        check_vma=False,
    )
```

```python
import jax
import jax.numpy as jnp
from jax import lax
from jax.experimental import pallas as pl
from jax.experimental.pallas import tpu as pltpu
from jax.sharding import Mesh
from jax.sharding import PartitionSpec as P

VIEW = ("vz", "vx")


def light_prefix(value):
    count = lax.axis_size("light")
    cells, columns = value.shape
    chunks = value.reshape(cells, count, columns // count).transpose(1, 0, 2)
    mine = lax.all_to_all(chunks, "light", 0, 0)
    running = jnp.cumsum(mine, axis=0)
    before = jnp.concatenate([jnp.zeros_like(running[:1]), running[:-1]], axis=0)
    back = lax.all_to_all(before, "light", 0, 0)
    return back.transpose(1, 0, 2).reshape(cells, columns)


def shade_kernel(facing_ref, dens_ref, emit_ref, out_ref, part_ref, *, light_scale, view_scale):
    rows, cells, _ = dens_ref.shape
    blocks, width = out_ref.shape[0], out_ref.shape[-1]

    def row(l, depth):
        dens = dens_ref[l]
        emit = emit_ref[l]
        tau_light = dens * light_scale
        step = jnp.exp(-(dens * view_scale))
        base = emit * (1.0 - step)
        shaded = base * jnp.exp(-depth)
        s = [step[v:v + 1] for v in range(cells)]
        flip = facing_ref[l] == 1
        ahead = [None] * cells
        behind = [None] * cells
        ahead[0] = jnp.ones_like(s[0])
        for v in range(1, cells):
            ahead[v] = ahead[v - 1] * s[v - 1]
        behind[cells - 1] = jnp.ones_like(s[0])
        for v in range(cells - 2, -1, -1):
            behind[v] = behind[v + 1] * s[v + 1]
        weight = [jnp.where(flip, behind[v], ahead[v]) for v in range(cells)]
        flat = weight[0] * base[0:1]
        for v in range(1, cells):
            flat = flat + weight[v] * base[v:v + 1]
        trans = ahead[cells - 1] * s[cells - 1]
        for b in range(blocks):
            cut = slice(b * width, (b + 1) * width)
            out_ref[b, 0, 0, pl.ds(l, 1), :] = 0.2 * flat[:, cut]
            out_ref[b, 1, 0, pl.ds(l, 1), :] = trans[:, cut]
            for v in range(cells):
                part_ref[v, b, 0, pl.ds(l, 1), :] = (weight[v] * shaded[v:v + 1])[:, cut]
        return depth + tau_light

    lax.fori_loop(0, rows, row, jnp.zeros(dens_ref.shape[1:], jnp.float32), unroll=8)


def shade(facing, density, emission, light_scale, view_scale, blocks, width):
    rows, cells, columns = density.shape
    tile = blocks * width
    tiles = columns // tile
    body = lambda *refs: shade_kernel(*refs, light_scale=light_scale, view_scale=view_scale)
    return pl.pallas_call(
        body,
        grid=(tiles,),
        in_specs=[
            pl.BlockSpec(memory_space=pltpu.SMEM),
            pl.BlockSpec((rows, cells, tile), lambda j: (0, 0, j)),
            pl.BlockSpec((rows, cells, tile), lambda j: (0, 0, j)),
        ],
        out_specs=[
            pl.BlockSpec((blocks, 2, 1, rows, width), lambda j: (0, 0, j, 0, 0)),
            pl.BlockSpec((cells, blocks, 1, rows, width), lambda j: (0, 0, j, 0, 0)),
        ],
        out_shape=[
            jax.ShapeDtypeStruct((blocks, 2, tiles, rows, width), jnp.float32),
            jax.ShapeDtypeStruct((cells, blocks, tiles, rows, width), jnp.float32),
        ],
        cost_estimate=pl.CostEstimate(
            flops=40 * density.size, transcendentals=2 * density.size, bytes_accessed=4 * 4 * density.size + 8 * rows * columns
        ),
    )(facing, density, emission)


def lit_kernel(light_ref, parts_ref, unshaded_ref, out_ref):
    total = unshaded_ref[:, 0]
    for v in range(parts_ref.shape[0]):
        total = total + light_ref[v] * parts_ref[v]
    out_ref[:, 0] = total


def apply_light(light, parts, unshaded):
    cells, blocks, tiles, rows, width = parts.shape
    return pl.pallas_call(
        lit_kernel,
        grid=(tiles,),
        in_specs=[
            pl.BlockSpec((cells, blocks, 1, 1, width), lambda j: (0, 0, j, 0, 0)),
            pl.BlockSpec((cells, blocks, 1, rows, width), lambda j: (0, 0, j, 0, 0)),
            pl.BlockSpec((blocks, 1, 1, rows, width), lambda j: (0, 0, j, 0, 0)),
        ],
        out_specs=pl.BlockSpec((blocks, 1, 1, rows, width), lambda j: (0, 0, j, 0, 0)),
        out_shape=jax.ShapeDtypeStruct(unshaded.shape, unshaded.dtype),
        input_output_aliases={2: 0},
        cost_estimate=pl.CostEstimate(
            flops=2 * parts.size, transcendentals=0, bytes_accessed=4 * (parts.size + 2 * blocks * tiles * rows * width)
        ),
    )(light, parts, unshaded)


def composite(colors, transes, reversed_rows):
    count = colors.shape[0]
    forward = colors[count - 1]
    for j in range(count - 2, -1, -1):
        forward = colors[j] + transes[j] * forward
    backward = colors[0]
    for j in range(1, count):
        backward = colors[j] + transes[j] * backward
    return jnp.where(reversed_rows, backward, forward)


def shards(density, emission, facing):
    rows, cells, columns = density.shape
    light_count = lax.axis_size("light")
    z_count = lax.axis_size("vz")
    x_count = lax.axis_size("vx")
    view_count = z_count * x_count
    tau_light = density * (1.0 / (rows * light_count))
    slab_depth = jnp.sum(tau_light, axis=0)
    reversed_rows = facing == 1
    width = columns // view_count
    unshaded, parts = shade(
        facing, density, emission, 1.0 / (rows * light_count), 1.0 / (cells * view_count), x_count, width
    )
    incoming = light_prefix(slab_depth)
    light = jnp.exp(-incoming).reshape(cells, z_count, x_count, 1, width).transpose(0, 2, 1, 3, 4)
    stacked = apply_light(light, parts, unshaded)
    along_x = lax.all_to_all(stacked, "vx", 0, 0)
    color_x = composite(along_x[:, 0], along_x[:, 1], reversed_rows[None, :, None])
    trans_x = jnp.prod(along_x[:, 1], axis=0)
    along_z = lax.all_to_all(jnp.stack([color_x, trans_x], axis=1), "vz", 0, 0)
    radiance = composite(along_z[:, 0], along_z[:, 1], reversed_rows[:, None])
    coverage = jnp.prod(along_z[:, 1], axis=0)
    return (radiance, coverage)


def view_split(mesh):
    row = mesh.devices.reshape(mesh.devices.shape[0], -1)[0]
    coords = [getattr(d, "coords", None) for d in row]
    if any(c is None for c in coords):
        return 1
    first_z = coords[0][2]
    return sum(1 for c in coords if c[2] == first_z)


def solution(mesh):
    x_count = view_split(mesh)
    light_count, view_count = mesh.devices.shape
    split = Mesh(mesh.devices.reshape(light_count, view_count // x_count, x_count), ("light",) + VIEW)
    return jax.shard_map(
        shards,
        mesh=split,
        in_specs=(P("light", VIEW, None), P("light", VIEW, None), P("light")),
        out_specs=(P("light", VIEW), P("light", VIEW)),
        check_vma=False,
    )
```

```python
import jax
import jax.numpy as jnp
from jax import lax
from jax.experimental import pallas as pl
from jax.experimental.pallas import tpu as pltpu
from jax.sharding import Mesh
from jax.sharding import PartitionSpec as P

VIEW = ("vz", "vx")


def light_prefix(value):
    count = lax.axis_size("light")
    cells, columns = value.shape
    chunks = value.reshape(cells, count, columns // count).transpose(1, 0, 2)
    mine = lax.all_to_all(chunks, "light", 0, 0)
    running = jnp.cumsum(mine, axis=0)
    before = jnp.concatenate([jnp.zeros_like(running[:1]), running[:-1]], axis=0)
    back = lax.all_to_all(before, "light", 0, 0)
    return back.transpose(1, 0, 2).reshape(cells, columns)


def shade_kernel(facing_ref, dens_ref, emit_ref, out_ref, part_ref, *, light_scale, view_scale):
    rows, cells, _ = dens_ref.shape
    blocks, width = out_ref.shape[0], out_ref.shape[-1]

    def row(l, depth):
        dens = dens_ref[l]
        emit = emit_ref[l]
        tau_light = dens * light_scale
        step = jnp.exp(-(dens * view_scale))
        base = emit * (1.0 - step)
        shaded = base * jnp.exp(-depth)
        s = [step[v:v + 1] for v in range(cells)]
        flip = facing_ref[l] == 1
        ahead = [None] * cells
        behind = [None] * cells
        ahead[0] = jnp.ones_like(s[0])
        for v in range(1, cells):
            ahead[v] = ahead[v - 1] * s[v - 1]
        behind[cells - 1] = jnp.ones_like(s[0])
        for v in range(cells - 2, -1, -1):
            behind[v] = behind[v + 1] * s[v + 1]
        weight = [jnp.where(flip, behind[v], ahead[v]) for v in range(cells)]
        flat = weight[0] * base[0:1]
        for v in range(1, cells):
            flat = flat + weight[v] * base[v:v + 1]
        trans = ahead[cells - 1] * s[cells - 1]
        for b in range(blocks):
            cut = slice(b * width, (b + 1) * width)
            out_ref[b, 0, 0, pl.ds(l, 1), :] = 0.2 * flat[:, cut]
            out_ref[b, 1, 0, pl.ds(l, 1), :] = trans[:, cut]
            for v in range(cells):
                part_ref[v, b, 0, pl.ds(l, 1), :] = (weight[v] * shaded[v:v + 1])[:, cut]
        return depth + tau_light

    lax.fori_loop(0, rows, row, jnp.zeros(dens_ref.shape[1:], jnp.float32), unroll=8)


def shade(facing, density, emission, light_scale, view_scale, blocks, width):
    rows, cells, columns = density.shape
    tile = blocks * width
    tiles = columns // tile
    body = lambda *refs: shade_kernel(*refs, light_scale=light_scale, view_scale=view_scale)
    return pl.pallas_call(
        body,
        grid=(tiles,),
        in_specs=[
            pl.BlockSpec(memory_space=pltpu.SMEM),
            pl.BlockSpec((rows, cells, tile), lambda j: (0, 0, j)),
            pl.BlockSpec((rows, cells, tile), lambda j: (0, 0, j)),
        ],
        out_specs=[
            pl.BlockSpec((blocks, 2, 1, rows, width), lambda j: (0, 0, j, 0, 0)),
            pl.BlockSpec((cells, blocks, 1, rows, width), lambda j: (0, 0, j, 0, 0)),
        ],
        out_shape=[
            jax.ShapeDtypeStruct((blocks, 2, tiles, rows, width), jnp.float32),
            jax.ShapeDtypeStruct((cells, blocks, tiles, rows, width), jnp.float32),
        ],
        cost_estimate=pl.CostEstimate(
            flops=40 * density.size, transcendentals=2 * density.size, bytes_accessed=4 * 4 * density.size + 8 * rows * columns
        ),
    )(facing, density, emission)


def lit_kernel(light_ref, parts_ref, unshaded_ref, out_ref):
    j = pl.program_id(0)
    total = unshaded_ref[:, 0]
    for v in range(parts_ref.shape[0]):
        total = total + light_ref[v, :, pl.ds(j, 1)] * parts_ref[v]
    out_ref[:, 0] = total


def apply_light(light, parts, unshaded):
    cells, blocks, tiles, rows, width = parts.shape
    return pl.pallas_call(
        lit_kernel,
        grid=(tiles,),
        in_specs=[
            pl.BlockSpec(light.shape, lambda j: (0, 0, 0, 0, 0)),
            pl.BlockSpec((cells, blocks, 1, rows, width), lambda j: (0, 0, j, 0, 0)),
            pl.BlockSpec((blocks, 1, 1, rows, width), lambda j: (0, 0, j, 0, 0)),
        ],
        out_specs=pl.BlockSpec((blocks, 1, 1, rows, width), lambda j: (0, 0, j, 0, 0)),
        out_shape=jax.ShapeDtypeStruct(unshaded.shape, unshaded.dtype),
        input_output_aliases={2: 0},
        cost_estimate=pl.CostEstimate(
            flops=2 * parts.size, transcendentals=0, bytes_accessed=4 * (parts.size + 2 * blocks * tiles * rows * width)
        ),
    )(light, parts, unshaded)


def composite(colors, transes, reversed_rows):
    count = colors.shape[0]
    forward = colors[count - 1]
    for j in range(count - 2, -1, -1):
        forward = colors[j] + transes[j] * forward
    backward = colors[0]
    for j in range(1, count):
        backward = colors[j] + transes[j] * backward
    return jnp.where(reversed_rows, backward, forward)


def shards(density, emission, facing):
    rows, cells, columns = density.shape
    light_count = lax.axis_size("light")
    z_count = lax.axis_size("vz")
    x_count = lax.axis_size("vx")
    view_count = z_count * x_count
    tau_light = density * (1.0 / (rows * light_count))
    slab_depth = jnp.sum(tau_light, axis=0)
    reversed_rows = facing == 1
    width = columns // view_count
    unshaded, parts = shade(
        facing, density, emission, 1.0 / (rows * light_count), 1.0 / (cells * view_count), x_count, width
    )
    incoming = light_prefix(slab_depth)
    light = jnp.exp(-incoming).reshape(cells, z_count, x_count, 1, width).transpose(0, 2, 1, 3, 4)
    stacked = apply_light(light, parts, unshaded)
    along_x = lax.all_to_all(stacked, "vx", 0, 0)
    color_x = composite(along_x[:, 0], along_x[:, 1], reversed_rows[None, :, None])
    trans_x = jnp.prod(along_x[:, 1], axis=0)
    along_z = lax.all_to_all(jnp.stack([color_x, trans_x], axis=1), "vz", 0, 0)
    radiance = composite(along_z[:, 0], along_z[:, 1], reversed_rows[:, None])
    coverage = jnp.prod(along_z[:, 1], axis=0)
    return (radiance, coverage)


def view_split(mesh):
    row = mesh.devices.reshape(mesh.devices.shape[0], -1)[0]
    coords = [getattr(d, "coords", None) for d in row]
    if any(c is None for c in coords):
        return 1
    first_z = coords[0][2]
    return sum(1 for c in coords if c[2] == first_z)


def solution(mesh):
    x_count = view_split(mesh)
    light_count, view_count = mesh.devices.shape
    split = Mesh(mesh.devices.reshape(light_count, view_count // x_count, x_count), ("light",) + VIEW)
    return jax.shard_map(
        shards,
        mesh=split,
        in_specs=(P("light", VIEW, None), P("light", VIEW, None), P("light")),
        out_specs=(P("light", VIEW), P("light", VIEW)),
        check_vma=False,
    )
```

```python
import jax
import jax.numpy as jnp
from jax import lax
from jax.experimental import pallas as pl
from jax.experimental.pallas import tpu as pltpu
from jax.sharding import Mesh
from jax.sharding import PartitionSpec as P

VIEW = ("vz", "vx")


def light_prefix(value):
    count = lax.axis_size("light")
    cells, columns = value.shape
    chunks = value.reshape(cells, count, columns // count).transpose(1, 0, 2)
    mine = lax.all_to_all(chunks, "light", 0, 0)
    running = jnp.cumsum(mine, axis=0)
    before = jnp.concatenate([jnp.zeros_like(running[:1]), running[:-1]], axis=0)
    back = lax.all_to_all(before, "light", 0, 0)
    return back.transpose(1, 0, 2).reshape(cells, columns)


def shade_kernel(facing_ref, dens_ref, emit_ref, out_ref, part_ref, *, light_scale, view_scale):
    rows, cells, _ = dens_ref.shape
    blocks, width = out_ref.shape[0], out_ref.shape[-1]

    def row(l, depth):
        dens = dens_ref[l]
        emit = emit_ref[l]
        tau_light = dens * light_scale
        step = jnp.exp(-(dens * view_scale))
        base = emit * (1.0 - step)
        shaded = base * jnp.exp(-depth)
        s = [step[v:v + 1] for v in range(cells)]
        flip = facing_ref[l] == 1
        ahead = [None] * cells
        behind = [None] * cells
        ahead[0] = jnp.ones_like(s[0])
        for v in range(1, cells):
            ahead[v] = ahead[v - 1] * s[v - 1]
        behind[cells - 1] = jnp.ones_like(s[0])
        for v in range(cells - 2, -1, -1):
            behind[v] = behind[v + 1] * s[v + 1]
        weight = [jnp.where(flip, behind[v], ahead[v]) for v in range(cells)]
        flat = weight[0] * base[0:1]
        for v in range(1, cells):
            flat = flat + weight[v] * base[v:v + 1]
        trans = ahead[cells - 1] * s[cells - 1]
        parts = [weight[v] * shaded[v:v + 1] for v in range(cells)]
        return depth + tau_light, [0.2 * flat, trans] + parts

    group = 8

    def rows_of(g, depth):
        first = pl.multiple_of(g * group, group)
        outs = []
        for k in range(group):
            depth, got = row(first + k, depth)
            outs.append(got)
        lines = [jnp.concatenate([o[i] for o in outs], axis=0) for i in range(2 + cells)]
        for b in range(blocks):
            cut = slice(b * width, (b + 1) * width)
            out_ref[b, 0, 0, pl.ds(first, group), :] = lines[0][:, cut]
            out_ref[b, 1, 0, pl.ds(first, group), :] = lines[1][:, cut]
            for v in range(cells):
                part_ref[v, b, 0, pl.ds(first, group), :] = lines[2 + v][:, cut]
        return depth

    lax.fori_loop(0, rows // group, rows_of, jnp.zeros(dens_ref.shape[1:], jnp.float32))


def shade(facing, density, emission, light_scale, view_scale, blocks, width):
    rows, cells, columns = density.shape
    tile = blocks * width
    tiles = columns // tile
    body = lambda *refs: shade_kernel(*refs, light_scale=light_scale, view_scale=view_scale)
    return pl.pallas_call(
        body,
        grid=(tiles,),
        in_specs=[
            pl.BlockSpec(memory_space=pltpu.SMEM),
            pl.BlockSpec((rows, cells, tile), lambda j: (0, 0, j)),
            pl.BlockSpec((rows, cells, tile), lambda j: (0, 0, j)),
        ],
        out_specs=[
            pl.BlockSpec((blocks, 2, 1, rows, width), lambda j: (0, 0, j, 0, 0)),
            pl.BlockSpec((cells, blocks, 1, rows, width), lambda j: (0, 0, j, 0, 0)),
        ],
        out_shape=[
            jax.ShapeDtypeStruct((blocks, 2, tiles, rows, width), jnp.float32),
            jax.ShapeDtypeStruct((cells, blocks, tiles, rows, width), jnp.float32),
        ],
        cost_estimate=pl.CostEstimate(
            flops=40 * density.size, transcendentals=2 * density.size, bytes_accessed=4 * 4 * density.size + 8 * rows * columns
        ),
    )(facing, density, emission)


def composite(colors, transes, reversed_rows):
    count = colors.shape[0]
    forward = colors[count - 1]
    for j in range(count - 2, -1, -1):
        forward = colors[j] + transes[j] * forward
    backward = colors[0]
    for j in range(1, count):
        backward = colors[j] + transes[j] * backward
    return jnp.where(reversed_rows, backward, forward)


def shards(density, emission, facing):
    rows, cells, columns = density.shape
    light_count = lax.axis_size("light")
    z_count = lax.axis_size("vz")
    x_count = lax.axis_size("vx")
    view_count = z_count * x_count
    tau_light = density * (1.0 / (rows * light_count))
    slab_depth = jnp.sum(tau_light, axis=0)
    reversed_rows = facing == 1
    width = columns // view_count
    unshaded, parts = shade(
        facing, density, emission, 1.0 / (rows * light_count), 1.0 / (cells * view_count), x_count, width
    )
    incoming = light_prefix(slab_depth)
    light = jnp.exp(-incoming).reshape(cells, z_count, x_count, 1, width).transpose(0, 2, 1, 3, 4)
    color = unshaded[:, 0] + jnp.sum(light * parts, axis=0)
    stacked = jnp.stack([color, unshaded[:, 1]], axis=1)
    along_x = lax.all_to_all(stacked, "vx", 0, 0)
    color_x = composite(along_x[:, 0], along_x[:, 1], reversed_rows[None, :, None])
    trans_x = jnp.prod(along_x[:, 1], axis=0)
    along_z = lax.all_to_all(jnp.stack([color_x, trans_x], axis=1), "vz", 0, 0)
    radiance = composite(along_z[:, 0], along_z[:, 1], reversed_rows[:, None])
    coverage = jnp.prod(along_z[:, 1], axis=0)
    return (radiance, coverage)


def view_split(mesh):
    row = mesh.devices.reshape(mesh.devices.shape[0], -1)[0]
    coords = [getattr(d, "coords", None) for d in row]
    if any(c is None for c in coords):
        return 1
    first_z = coords[0][2]
    return sum(1 for c in coords if c[2] == first_z)


def solution(mesh):
    x_count = view_split(mesh)
    light_count, view_count = mesh.devices.shape
    split = Mesh(mesh.devices.reshape(light_count, view_count // x_count, x_count), ("light",) + VIEW)
    return jax.shard_map(
        shards,
        mesh=split,
        in_specs=(P("light", VIEW, None), P("light", VIEW, None), P("light")),
        out_specs=(P("light", VIEW), P("light", VIEW)),
        check_vma=False,
    )
```

```python
import jax
import jax.numpy as jnp
from jax import lax
from jax.experimental import pallas as pl
from jax.experimental.pallas import tpu as pltpu
from jax.sharding import Mesh
from jax.sharding import PartitionSpec as P

VIEW = ("vz", "vx")


def light_prefix(value):
    count = lax.axis_size("light")
    cells, columns = value.shape
    chunks = value.reshape(cells, count, columns // count).transpose(1, 0, 2)
    mine = lax.all_to_all(chunks, "light", 0, 0)
    before = jnp.cumsum(mine, axis=0) - mine
    back = lax.all_to_all(before, "light", 0, 0)
    return back.transpose(1, 0, 2).reshape(cells, columns)


def shade_kernel(facing_ref, dens_ref, emit_ref, out_ref, part_ref, *, light_scale, view_scale):
    rows, cells, _ = dens_ref.shape
    blocks, width = out_ref.shape[0], out_ref.shape[-1]

    def row(l, depth):
        dens = dens_ref[l]
        emit = emit_ref[l]
        tau_light = dens * light_scale
        step = jnp.exp(-(dens * view_scale))
        base = emit * (1.0 - step)
        shaded = base * jnp.exp(-depth)
        s = [step[v:v + 1] for v in range(cells)]
        flip = facing_ref[l] == 1
        ahead = [None] * cells
        behind = [None] * cells
        ahead[0] = jnp.ones_like(s[0])
        for v in range(1, cells):
            ahead[v] = ahead[v - 1] * s[v - 1]
        behind[cells - 1] = jnp.ones_like(s[0])
        for v in range(cells - 2, -1, -1):
            behind[v] = behind[v + 1] * s[v + 1]
        weight = [jnp.where(flip, behind[v], ahead[v]) for v in range(cells)]
        flat = weight[0] * base[0:1]
        for v in range(1, cells):
            flat = flat + weight[v] * base[v:v + 1]
        trans = ahead[cells - 1] * s[cells - 1]
        for b in range(blocks):
            cut = slice(b * width, (b + 1) * width)
            out_ref[b, 0, 0, pl.ds(l, 1), :] = 0.2 * flat[:, cut]
            out_ref[b, 1, 0, pl.ds(l, 1), :] = trans[:, cut]
            for v in range(cells):
                part_ref[v, b, 0, pl.ds(l, 1), :] = (weight[v] * shaded[v:v + 1])[:, cut]
        return depth + tau_light

    lax.fori_loop(0, rows, row, jnp.zeros(dens_ref.shape[1:], jnp.float32), unroll=8)


def shade(facing, density, emission, light_scale, view_scale, blocks, width):
    rows, cells, columns = density.shape
    tile = blocks * width
    tiles = columns // tile
    body = lambda *refs: shade_kernel(*refs, light_scale=light_scale, view_scale=view_scale)
    return pl.pallas_call(
        body,
        grid=(tiles,),
        in_specs=[
            pl.BlockSpec(memory_space=pltpu.SMEM),
            pl.BlockSpec((rows, cells, tile), lambda j: (0, 0, j)),
            pl.BlockSpec((rows, cells, tile), lambda j: (0, 0, j)),
        ],
        out_specs=[
            pl.BlockSpec((blocks, 2, 1, rows, width), lambda j: (0, 0, j, 0, 0)),
            pl.BlockSpec((cells, blocks, 1, rows, width), lambda j: (0, 0, j, 0, 0)),
        ],
        out_shape=[
            jax.ShapeDtypeStruct((blocks, 2, tiles, rows, width), jnp.float32),
            jax.ShapeDtypeStruct((cells, blocks, tiles, rows, width), jnp.float32),
        ],
        cost_estimate=pl.CostEstimate(
            flops=40 * density.size, transcendentals=2 * density.size, bytes_accessed=4 * 4 * density.size + 8 * rows * columns
        ),
    )(facing, density, emission)


def composite(colors, transes, reversed_rows):
    count = colors.shape[0]
    forward = colors[count - 1]
    for j in range(count - 2, -1, -1):
        forward = colors[j] + transes[j] * forward
    backward = colors[0]
    for j in range(1, count):
        backward = colors[j] + transes[j] * backward
    return jnp.where(reversed_rows, backward, forward)


def shards(density, emission, facing):
    rows, cells, columns = density.shape
    light_count = lax.axis_size("light")
    z_count = lax.axis_size("vz")
    x_count = lax.axis_size("vx")
    view_count = z_count * x_count
    tau_light = density * (1.0 / (rows * light_count))
    slab_depth = jnp.sum(tau_light, axis=0)
    reversed_rows = facing == 1
    width = columns // view_count
    unshaded, parts = shade(
        facing, density, emission, 1.0 / (rows * light_count), 1.0 / (cells * view_count), x_count, width
    )
    incoming = light_prefix(slab_depth)
    light = jnp.exp(-incoming).reshape(cells, z_count, x_count, 1, width).transpose(0, 2, 1, 3, 4)
    color = unshaded[:, 0] + jnp.sum(light * parts, axis=0)
    stacked = jnp.stack([color, unshaded[:, 1]], axis=1)
    along_x = lax.all_to_all(stacked, "vx", 0, 0)
    color_x = composite(along_x[:, 0], along_x[:, 1], reversed_rows[None, :, None])
    trans_x = jnp.prod(along_x[:, 1], axis=0)
    along_z = lax.all_to_all(jnp.stack([color_x, trans_x], axis=1), "vz", 0, 0)
    radiance = composite(along_z[:, 0], along_z[:, 1], reversed_rows[:, None])
    coverage = jnp.prod(along_z[:, 1], axis=0)
    return (radiance, coverage)


def view_split(mesh):
    row = mesh.devices.reshape(mesh.devices.shape[0], -1)[0]
    coords = [getattr(d, "coords", None) for d in row]
    if any(c is None for c in coords):
        return 1
    first_z = coords[0][2]
    return sum(1 for c in coords if c[2] == first_z)


def solution(mesh):
    x_count = view_split(mesh)
    light_count, view_count = mesh.devices.shape
    split = Mesh(mesh.devices.reshape(light_count, view_count // x_count, x_count), ("light",) + VIEW)
    return jax.shard_map(
        shards,
        mesh=split,
        in_specs=(P("light", VIEW, None), P("light", VIEW, None), P("light")),
        out_specs=(P("light", VIEW), P("light", VIEW)),
        check_vma=False,
    )
```

```python
import jax
import jax.numpy as jnp
from jax import lax
from jax.experimental import pallas as pl
from jax.experimental.pallas import tpu as pltpu
from jax.sharding import Mesh
from jax.sharding import PartitionSpec as P

VIEW = ("vz", "vx")


def light_prefix(value):
    count = lax.axis_size("light")
    cells, columns = value.shape
    chunks = value.reshape(cells, count, columns // count).transpose(1, 0, 2)
    mine = lax.all_to_all(chunks, "light", 0, 0)
    before = jnp.cumsum(mine, axis=0) - mine
    back = lax.all_to_all(before, "light", 0, 0)
    return back.transpose(1, 0, 2).reshape(cells, columns)


def shade_kernel(facing_ref, dens_ref, emit_ref, out_ref, part_ref, *, light_scale, view_scale):
    rows, cells, _ = dens_ref.shape
    blocks, width = out_ref.shape[0], out_ref.shape[-1]

    def row(l, depth):
        dens = dens_ref[l]
        emit = emit_ref[l]
        tau_light = dens * light_scale
        step = jnp.exp(-(dens * view_scale))
        base = emit * (1.0 - step)
        shaded = base * jnp.exp(-depth)
        s = [step[v:v + 1] for v in range(cells)]
        flip = facing_ref[l] == 1
        ahead = [None] * cells
        behind = [None] * cells
        ahead[0] = jnp.ones_like(s[0])
        for v in range(1, cells):
            ahead[v] = ahead[v - 1] * s[v - 1]
        behind[cells - 1] = jnp.ones_like(s[0])
        for v in range(cells - 2, -1, -1):
            behind[v] = behind[v + 1] * s[v + 1]
        weight = [jnp.where(flip, behind[v], ahead[v]) for v in range(cells)]
        flat = weight[0] * base[0:1]
        for v in range(1, cells):
            flat = flat + weight[v] * base[v:v + 1]
        trans = ahead[cells - 1] * s[cells - 1]
        for b in range(blocks):
            cut = slice(b * width, (b + 1) * width)
            out_ref[b, 0, 0, pl.ds(l, 1), :] = 0.2 * flat[:, cut]
            out_ref[b, 1, 0, pl.ds(l, 1), :] = trans[:, cut]
            for v in range(cells):
                part_ref[v, b, 0, pl.ds(l, 1), :] = (weight[v] * shaded[v:v + 1])[:, cut]
        return depth + tau_light

    lax.fori_loop(0, rows, row, jnp.zeros(dens_ref.shape[1:], jnp.float32), unroll=8)


def shade(facing, density, emission, light_scale, view_scale, blocks, width):
    rows, cells, columns = density.shape
    tile = blocks * width
    tiles = columns // tile
    body = lambda *refs: shade_kernel(*refs, light_scale=light_scale, view_scale=view_scale)
    return pl.pallas_call(
        body,
        grid=(tiles,),
        in_specs=[
            pl.BlockSpec(memory_space=pltpu.SMEM),
            pl.BlockSpec((rows, cells, tile), lambda j: (0, 0, j)),
            pl.BlockSpec((rows, cells, tile), lambda j: (0, 0, j)),
        ],
        out_specs=[
            pl.BlockSpec((blocks, 2, 1, rows, width), lambda j: (0, 0, j, 0, 0)),
            pl.BlockSpec((cells, blocks, 1, rows, width), lambda j: (0, 0, j, 0, 0)),
        ],
        out_shape=[
            jax.ShapeDtypeStruct((blocks, 2, tiles, rows, width), jnp.float32),
            jax.ShapeDtypeStruct((cells, blocks, tiles, rows, width), jnp.float32),
        ],
        cost_estimate=pl.CostEstimate(
            flops=40 * density.size, transcendentals=2 * density.size, bytes_accessed=4 * 4 * density.size + 8 * rows * columns
        ),
    )(facing, density, emission)


def slab_kernel(dens_ref, out_ref, *, light_scale):
    total = dens_ref[0] * light_scale
    for l in range(1, dens_ref.shape[0]):
        total = total + dens_ref[l] * light_scale
    out_ref[...] = total


def slab_depth_of(density, light_scale, tile=1024):
    rows, cells, columns = density.shape
    tile = min(tile, columns)
    return pl.pallas_call(
        lambda d, o: slab_kernel(d, o, light_scale=light_scale),
        grid=(columns // tile,),
        in_specs=[pl.BlockSpec((rows, cells, tile), lambda j: (0, 0, j))],
        out_specs=pl.BlockSpec((cells, tile), lambda j: (0, j)),
        out_shape=jax.ShapeDtypeStruct((cells, columns), jnp.float32),
        cost_estimate=pl.CostEstimate(flops=2 * density.size, transcendentals=0, bytes_accessed=4 * density.size),
    )(density)


def composite(colors, transes, reversed_rows):
    count = colors.shape[0]
    forward = colors[count - 1]
    for j in range(count - 2, -1, -1):
        forward = colors[j] + transes[j] * forward
    backward = colors[0]
    for j in range(1, count):
        backward = colors[j] + transes[j] * backward
    return jnp.where(reversed_rows, backward, forward)


def shards(density, emission, facing):
    rows, cells, columns = density.shape
    light_count = lax.axis_size("light")
    z_count = lax.axis_size("vz")
    x_count = lax.axis_size("vx")
    view_count = z_count * x_count
    slab_depth = slab_depth_of(density, 1.0 / (rows * light_count))
    reversed_rows = facing == 1
    width = columns // view_count
    unshaded, parts = shade(
        facing, density, emission, 1.0 / (rows * light_count), 1.0 / (cells * view_count), x_count, width
    )
    incoming = light_prefix(slab_depth)
    light = jnp.exp(-incoming).reshape(cells, z_count, x_count, 1, width).transpose(0, 2, 1, 3, 4)
    color = unshaded[:, 0] + jnp.sum(light * parts, axis=0)
    stacked = jnp.stack([color, unshaded[:, 1]], axis=1)
    along_x = lax.all_to_all(stacked, "vx", 0, 0)
    color_x = composite(along_x[:, 0], along_x[:, 1], reversed_rows[None, :, None])
    trans_x = jnp.prod(along_x[:, 1], axis=0)
    along_z = lax.all_to_all(jnp.stack([color_x, trans_x], axis=1), "vz", 0, 0)
    radiance = composite(along_z[:, 0], along_z[:, 1], reversed_rows[:, None])
    coverage = jnp.prod(along_z[:, 1], axis=0)
    return (radiance, coverage)


def view_split(mesh):
    row = mesh.devices.reshape(mesh.devices.shape[0], -1)[0]
    coords = [getattr(d, "coords", None) for d in row]
    if any(c is None for c in coords):
        return 1
    first_z = coords[0][2]
    return sum(1 for c in coords if c[2] == first_z)


def solution(mesh):
    x_count = view_split(mesh)
    light_count, view_count = mesh.devices.shape
    split = Mesh(mesh.devices.reshape(light_count, view_count // x_count, x_count), ("light",) + VIEW)
    return jax.shard_map(
        shards,
        mesh=split,
        in_specs=(P("light", VIEW, None), P("light", VIEW, None), P("light")),
        out_specs=(P("light", VIEW), P("light", VIEW)),
        check_vma=False,
    )
```

```python
import jax
import jax.numpy as jnp
from jax import lax
from jax.experimental import pallas as pl
from jax.experimental.pallas import tpu as pltpu
from jax.sharding import Mesh
from jax.sharding import PartitionSpec as P

VIEW = ("vz", "vx")


def light_prefix(value):
    count = lax.axis_size("light")
    cells, columns = value.shape
    chunks = value.reshape(cells, count, columns // count).transpose(1, 0, 2)
    mine = lax.all_to_all(chunks, "light", 0, 0)
    before = jnp.cumsum(mine, axis=0) - mine
    back = lax.all_to_all(before, "light", 0, 0)
    return back.transpose(1, 0, 2).reshape(cells, columns)


def shade_kernel(facing_ref, dens_ref, emit_ref, out_ref, part_ref, *, light_scale, view_scale):
    rows, cells, _ = dens_ref.shape
    blocks, width = out_ref.shape[0], out_ref.shape[-1]

    def row(l, depth):
        dens = dens_ref[l]
        emit = emit_ref[l]
        tau_light = dens * light_scale
        step = jnp.exp(-(dens * view_scale))
        base = emit * (1.0 - step)
        shaded = base * jnp.exp(-depth)
        s = [step[v:v + 1] for v in range(cells)]
        flip = facing_ref[l] == 1
        ahead = [None] * cells
        behind = [None] * cells
        ahead[0] = jnp.ones_like(s[0])
        for v in range(1, cells):
            ahead[v] = ahead[v - 1] * s[v - 1]
        behind[cells - 1] = jnp.ones_like(s[0])
        for v in range(cells - 2, -1, -1):
            behind[v] = behind[v + 1] * s[v + 1]
        weight = [jnp.where(flip, behind[v], ahead[v]) for v in range(cells)]
        flat = weight[0] * base[0:1]
        for v in range(1, cells):
            flat = flat + weight[v] * base[v:v + 1]
        trans = ahead[cells - 1] * s[cells - 1]
        for b in range(blocks):
            cut = slice(b * width, (b + 1) * width)
            out_ref[b, 0, 0, pl.ds(l, 1), :] = 0.2 * flat[:, cut]
            out_ref[b, 1, 0, pl.ds(l, 1), :] = trans[:, cut]
            for v in range(cells):
                part_ref[v, b, 0, pl.ds(l, 1), :] = (weight[v] * shaded[v:v + 1])[:, cut]
        return depth + tau_light

    lax.fori_loop(0, rows, row, jnp.zeros(dens_ref.shape[1:], jnp.float32), unroll=True)


def shade(facing, density, emission, light_scale, view_scale, blocks, width):
    rows, cells, columns = density.shape
    tile = blocks * width
    tiles = columns // tile
    body = lambda *refs: shade_kernel(*refs, light_scale=light_scale, view_scale=view_scale)
    return pl.pallas_call(
        body,
        grid=(tiles,),
        in_specs=[
            pl.BlockSpec(memory_space=pltpu.SMEM),
            pl.BlockSpec((rows, cells, tile), lambda j: (0, 0, j)),
            pl.BlockSpec((rows, cells, tile), lambda j: (0, 0, j)),
        ],
        out_specs=[
            pl.BlockSpec((blocks, 2, 1, rows, width), lambda j: (0, 0, j, 0, 0)),
            pl.BlockSpec((cells, blocks, 1, rows, width), lambda j: (0, 0, j, 0, 0)),
        ],
        out_shape=[
            jax.ShapeDtypeStruct((blocks, 2, tiles, rows, width), jnp.float32),
            jax.ShapeDtypeStruct((cells, blocks, tiles, rows, width), jnp.float32),
        ],
        cost_estimate=pl.CostEstimate(
            flops=40 * density.size, transcendentals=2 * density.size, bytes_accessed=4 * 4 * density.size + 8 * rows * columns
        ),
    )(facing, density, emission)


def composite(colors, transes, reversed_rows):
    count = colors.shape[0]
    forward = colors[count - 1]
    for j in range(count - 2, -1, -1):
        forward = colors[j] + transes[j] * forward
    backward = colors[0]
    for j in range(1, count):
        backward = colors[j] + transes[j] * backward
    return jnp.where(reversed_rows, backward, forward)


def shards(density, emission, facing):
    rows, cells, columns = density.shape
    light_count = lax.axis_size("light")
    z_count = lax.axis_size("vz")
    x_count = lax.axis_size("vx")
    view_count = z_count * x_count
    tau_light = density * (1.0 / (rows * light_count))
    slab_depth = jnp.sum(tau_light, axis=0)
    reversed_rows = facing == 1
    width = columns // view_count
    unshaded, parts = shade(
        facing, density, emission, 1.0 / (rows * light_count), 1.0 / (cells * view_count), x_count, width
    )
    incoming = light_prefix(slab_depth)
    light = jnp.exp(-incoming).reshape(cells, z_count, x_count, 1, width).transpose(0, 2, 1, 3, 4)
    color = unshaded[:, 0] + jnp.sum(light * parts, axis=0)
    stacked = jnp.stack([color, unshaded[:, 1]], axis=1)
    along_x = lax.all_to_all(stacked, "vx", 0, 0)
    color_x = composite(along_x[:, 0], along_x[:, 1], reversed_rows[None, :, None])
    trans_x = jnp.prod(along_x[:, 1], axis=0)
    along_z = lax.all_to_all(jnp.stack([color_x, trans_x], axis=1), "vz", 0, 0)
    radiance = composite(along_z[:, 0], along_z[:, 1], reversed_rows[:, None])
    coverage = jnp.prod(along_z[:, 1], axis=0)
    return (radiance, coverage)


def view_split(mesh):
    row = mesh.devices.reshape(mesh.devices.shape[0], -1)[0]
    coords = [getattr(d, "coords", None) for d in row]
    if any(c is None for c in coords):
        return 1
    first_z = coords[0][2]
    return sum(1 for c in coords if c[2] == first_z)


def solution(mesh):
    x_count = view_split(mesh)
    light_count, view_count = mesh.devices.shape
    split = Mesh(mesh.devices.reshape(light_count, view_count // x_count, x_count), ("light",) + VIEW)
    return jax.shard_map(
        shards,
        mesh=split,
        in_specs=(P("light", VIEW, None), P("light", VIEW, None), P("light")),
        out_specs=(P("light", VIEW), P("light", VIEW)),
        check_vma=False,
    )
```

```python
import jax
import jax.numpy as jnp
from jax import lax
from jax.experimental import pallas as pl
from jax.experimental.pallas import tpu as pltpu
from jax.sharding import Mesh
from jax.sharding import PartitionSpec as P

VIEW = ("vz", "vx")


def light_prefix(value):
    count = lax.axis_size("light")
    cells, columns = value.shape
    chunks = value.reshape(cells, count, columns // count).transpose(1, 0, 2)
    mine = lax.all_to_all(chunks, "light", 0, 0)
    before = jnp.cumsum(mine, axis=0) - mine
    back = lax.all_to_all(before, "light", 0, 0)
    return back.transpose(1, 0, 2).reshape(cells, columns)


def shade_kernel(facing_ref, dens_ref, emit_ref, out_ref, part_ref, *, light_scale, view_scale):
    rows, cells, _ = dens_ref.shape
    blocks, width = out_ref.shape[0], out_ref.shape[-1]

    def row(l, depth):
        dens = dens_ref[l]
        emit = emit_ref[l]
        tau_light = dens * light_scale
        step = jnp.exp(-(dens * view_scale))
        base = emit * (1.0 - step)
        shaded = base * jnp.exp(-depth)
        s = [step[v:v + 1] for v in range(cells)]
        flip = facing_ref[l] == 1
        ahead = [None] * cells
        behind = [None] * cells
        ahead[0] = jnp.ones_like(s[0])
        for v in range(1, cells):
            ahead[v] = ahead[v - 1] * s[v - 1]
        behind[cells - 1] = jnp.ones_like(s[0])
        for v in range(cells - 2, -1, -1):
            behind[v] = behind[v + 1] * s[v + 1]
        weight = [jnp.where(flip, behind[v], ahead[v]) for v in range(cells)]
        flat = weight[0] * base[0:1]
        for v in range(1, cells):
            flat = flat + weight[v] * base[v:v + 1]
        trans = ahead[cells - 1] * s[cells - 1]
        for b in range(blocks):
            cut = slice(b * width, (b + 1) * width)
            out_ref[b, 0, 0, pl.ds(l, 1), :] = 0.2 * flat[:, cut]
            out_ref[b, 1, 0, pl.ds(l, 1), :] = trans[:, cut]
            for v in range(cells):
                part_ref[v, b, 0, pl.ds(l, 1), :] = (weight[v] * shaded[v:v + 1])[:, cut]
        return depth + tau_light

    lax.fori_loop(0, rows, row, jnp.zeros(dens_ref.shape[1:], jnp.float32), unroll=8)


def shade(facing, density, emission, light_scale, view_scale, blocks, width):
    rows, cells, columns = density.shape
    tile = blocks * width
    tiles = columns // tile
    body = lambda *refs: shade_kernel(*refs, light_scale=light_scale, view_scale=view_scale)
    return pl.pallas_call(
        body,
        grid=(tiles,),
        in_specs=[
            pl.BlockSpec(memory_space=pltpu.SMEM),
            pl.BlockSpec((rows, cells, tile), lambda j: (0, 0, j)),
            pl.BlockSpec((rows, cells, tile), lambda j: (0, 0, j)),
        ],
        out_specs=[
            pl.BlockSpec((blocks, 2, 1, rows, width), lambda j: (0, 0, j, 0, 0)),
            pl.BlockSpec((cells, blocks, 1, rows, width), lambda j: (0, 0, j, 0, 0)),
        ],
        out_shape=[
            jax.ShapeDtypeStruct((blocks, 2, tiles, rows, width), jnp.float32),
            jax.ShapeDtypeStruct((cells, blocks, tiles, rows, width), jnp.float32),
        ],
        cost_estimate=pl.CostEstimate(
            flops=40 * density.size, transcendentals=2 * density.size, bytes_accessed=4 * 4 * density.size + 8 * rows * columns
        ),
    )(facing, density, emission)


def lit_kernel(light_ref, parts_ref, unshaded_ref, out_ref):
    b = pl.program_id(0)
    total = unshaded_ref[0, 0]
    for v in range(parts_ref.shape[0]):
        total = total + light_ref[v, b] * parts_ref[v, 0]
    out_ref[0, 0] = total


def apply_light(light, parts, unshaded):
    cells, blocks, tiles, rows, width = parts.shape
    return pl.pallas_call(
        lit_kernel,
        grid=(blocks,),
        in_specs=[
            pl.BlockSpec(light.shape, lambda b: (0, 0, 0, 0, 0)),
            pl.BlockSpec((cells, 1, tiles, rows, width), lambda b: (0, b, 0, 0, 0)),
            pl.BlockSpec((1, 1, tiles, rows, width), lambda b: (b, 0, 0, 0, 0)),
        ],
        out_specs=pl.BlockSpec((1, 1, tiles, rows, width), lambda b: (b, 0, 0, 0, 0)),
        out_shape=jax.ShapeDtypeStruct(unshaded.shape, unshaded.dtype),
        input_output_aliases={2: 0},
        cost_estimate=pl.CostEstimate(
            flops=2 * parts.size, transcendentals=0, bytes_accessed=4 * (parts.size + 2 * blocks * tiles * rows * width)
        ),
    )(light, parts, unshaded)


def composite(colors, transes, reversed_rows):
    count = colors.shape[0]
    forward = colors[count - 1]
    for j in range(count - 2, -1, -1):
        forward = colors[j] + transes[j] * forward
    backward = colors[0]
    for j in range(1, count):
        backward = colors[j] + transes[j] * backward
    return jnp.where(reversed_rows, backward, forward)


def shards(density, emission, facing):
    rows, cells, columns = density.shape
    light_count = lax.axis_size("light")
    z_count = lax.axis_size("vz")
    x_count = lax.axis_size("vx")
    view_count = z_count * x_count
    tau_light = density * (1.0 / (rows * light_count))
    slab_depth = jnp.sum(tau_light, axis=0)
    reversed_rows = facing == 1
    width = columns // view_count
    unshaded, parts = shade(
        facing, density, emission, 1.0 / (rows * light_count), 1.0 / (cells * view_count), x_count, width
    )
    incoming = light_prefix(slab_depth)
    light = jnp.exp(-incoming).reshape(cells, z_count, x_count, 1, width).transpose(0, 2, 1, 3, 4)
    stacked = apply_light(light, parts, unshaded)
    along_x = lax.all_to_all(stacked, "vx", 0, 0)
    color_x = composite(along_x[:, 0], along_x[:, 1], reversed_rows[None, :, None])
    trans_x = jnp.prod(along_x[:, 1], axis=0)
    along_z = lax.all_to_all(jnp.stack([color_x, trans_x], axis=1), "vz", 0, 0)
    radiance = composite(along_z[:, 0], along_z[:, 1], reversed_rows[:, None])
    coverage = jnp.prod(along_z[:, 1], axis=0)
    return (radiance, coverage)


def view_split(mesh):
    row = mesh.devices.reshape(mesh.devices.shape[0], -1)[0]
    coords = [getattr(d, "coords", None) for d in row]
    if any(c is None for c in coords):
        return 1
    first_z = coords[0][2]
    return sum(1 for c in coords if c[2] == first_z)


def solution(mesh):
    x_count = view_split(mesh)
    light_count, view_count = mesh.devices.shape
    split = Mesh(mesh.devices.reshape(light_count, view_count // x_count, x_count), ("light",) + VIEW)
    return jax.shard_map(
        shards,
        mesh=split,
        in_specs=(P("light", VIEW, None), P("light", VIEW, None), P("light")),
        out_specs=(P("light", VIEW), P("light", VIEW)),
        check_vma=False,
    )
```

```python
import jax
import jax.numpy as jnp
from jax import lax
from jax.experimental import pallas as pl
from jax.experimental.pallas import tpu as pltpu
from jax.sharding import Mesh
from jax.sharding import PartitionSpec as P

VIEW = ("vz", "vx")


def light_prefix(value):
    count = lax.axis_size("light")
    cells, columns = value.shape
    chunks = value.reshape(cells, count, columns // count).transpose(1, 0, 2)
    mine = lax.all_to_all(chunks, "light", 0, 0)
    before = jnp.cumsum(mine, axis=0) - mine
    back = lax.all_to_all(before, "light", 0, 0)
    return back.transpose(1, 0, 2).reshape(cells, columns)


def shade_kernel(facing_ref, dens_ref, emit_ref, out_ref, part_ref, *, light_scale, view_scale):
    rows, cells, _ = dens_ref.shape
    blocks, width = out_ref.shape[0], out_ref.shape[-1]

    def row(l, depth):
        dens = dens_ref[l]
        emit = emit_ref[l]
        tau_light = dens * light_scale
        step = jnp.exp(-(dens * view_scale))
        base = emit * (1.0 - step)
        shaded = base * jnp.exp(-depth)
        s = [step[v:v + 1] for v in range(cells)]
        flip = facing_ref[l] == 1
        ahead = [None] * cells
        behind = [None] * cells
        ahead[0] = jnp.ones_like(s[0])
        for v in range(1, cells):
            ahead[v] = ahead[v - 1] * s[v - 1]
        behind[cells - 1] = jnp.ones_like(s[0])
        for v in range(cells - 2, -1, -1):
            behind[v] = behind[v + 1] * s[v + 1]
        weight = [jnp.where(flip, behind[v], ahead[v]) for v in range(cells)]
        flat = weight[0] * base[0:1]
        for v in range(1, cells):
            flat = flat + weight[v] * base[v:v + 1]
        trans = ahead[cells - 1] * s[cells - 1]
        for b in range(blocks):
            cut = slice(b * width, (b + 1) * width)
            out_ref[b, 0, 0, pl.ds(l, 1), :] = 0.2 * flat[:, cut]
            out_ref[b, 1, 0, pl.ds(l, 1), :] = trans[:, cut]
            for v in range(cells):
                part_ref[v, b, 0, pl.ds(l, 1), :] = (weight[v] * shaded[v:v + 1])[:, cut]
        return depth + tau_light

    lax.fori_loop(0, rows, row, jnp.zeros(dens_ref.shape[1:], jnp.float32), unroll=8)


def shade(facing, density, emission, light_scale, view_scale, blocks, width):
    rows, cells, columns = density.shape
    tile = blocks * width
    tiles = columns // tile
    body = lambda *refs: shade_kernel(*refs, light_scale=light_scale, view_scale=view_scale)
    return pl.pallas_call(
        body,
        grid=(tiles,),
        in_specs=[
            pl.BlockSpec(memory_space=pltpu.SMEM),
            pl.BlockSpec((rows, cells, tile), lambda j: (0, 0, j)),
            pl.BlockSpec((rows, cells, tile), lambda j: (0, 0, j)),
        ],
        out_specs=[
            pl.BlockSpec((blocks, 2, 1, rows, width), lambda j: (0, 0, j, 0, 0)),
            pl.BlockSpec((cells, blocks, 1, rows, width), lambda j: (0, 0, j, 0, 0)),
        ],
        out_shape=[
            jax.ShapeDtypeStruct((blocks, 2, tiles, rows, width), jnp.float32),
            jax.ShapeDtypeStruct((cells, blocks, tiles, rows, width), jnp.float32),
        ],
        cost_estimate=pl.CostEstimate(
            flops=40 * density.size, transcendentals=2 * density.size, bytes_accessed=4 * 4 * density.size + 8 * rows * columns
        ),
    )(facing, density, emission)


def composite(colors, transes, reversed_rows):
    count = colors.shape[0]
    forward = colors[count - 1]
    for j in range(count - 2, -1, -1):
        forward = colors[j] + transes[j] * forward
    backward = colors[0]
    for j in range(1, count):
        backward = colors[j] + transes[j] * backward
    return jnp.where(reversed_rows, backward, forward)


def shards(density, emission, facing):
    rows, cells, columns = density.shape
    light_count = lax.axis_size("light")
    z_count = lax.axis_size("vz")
    x_count = lax.axis_size("vx")
    view_count = z_count * x_count
    tau_light = density * (1.0 / (rows * light_count))
    slab_depth = jnp.sum(tau_light, axis=0)
    reversed_rows = facing == 1
    width = columns // view_count
    unshaded, parts = shade(
        facing, density, emission, 1.0 / (rows * light_count), 1.0 / (cells * view_count), x_count, width
    )
    incoming = light_prefix(slab_depth)
    light = jnp.exp(-incoming).reshape(cells, z_count, x_count, 1, width).transpose(0, 2, 1, 3, 4)
    color = unshaded[:, 0] + jnp.sum(light * parts, axis=0)
    stacked = jnp.stack([color, unshaded[:, 1]], axis=1)
    along_x = lax.all_to_all(stacked, "vx", 0, 0)
    color_x = composite(along_x[:, 0], along_x[:, 1], reversed_rows[None, :, None])
    trans_x = jnp.prod(along_x[:, 1], axis=0)
    along_z = lax.all_to_all(jnp.stack([color_x, trans_x], axis=1), "vz", 0, 0)
    radiance = composite(along_z[:, 0], along_z[:, 1], reversed_rows[:, None])
    coverage = jnp.prod(along_z[:, 1], axis=0)
    return (radiance, coverage)


def view_split(mesh):
    row = mesh.devices.reshape(mesh.devices.shape[0], -1)[0]
    coords = [getattr(d, "coords", None) for d in row]
    if any(c is None for c in coords):
        return 1
    first_z = coords[0][2]
    x_extent = sum(1 for c in coords if c[2] == first_z)
    return 2 * x_extent if len(row) % (2 * x_extent) == 0 else x_extent


def solution(mesh):
    x_count = view_split(mesh)
    light_count, view_count = mesh.devices.shape
    split = Mesh(mesh.devices.reshape(light_count, view_count // x_count, x_count), ("light",) + VIEW)
    return jax.shard_map(
        shards,
        mesh=split,
        in_specs=(P("light", VIEW, None), P("light", VIEW, None), P("light")),
        out_specs=(P("light", VIEW), P("light", VIEW)),
        check_vma=False,
    )
```

```python
import jax
import jax.numpy as jnp
from jax import lax
from jax.experimental import pallas as pl
from jax.experimental.pallas import tpu as pltpu
from jax.sharding import Mesh
from jax.sharding import PartitionSpec as P

VIEW = ("vz", "vx")


def light_prefix(value):
    count = lax.axis_size("light")
    cells, columns = value.shape
    chunks = value.reshape(cells, count, columns // count).transpose(1, 0, 2)
    mine = lax.all_to_all(chunks, "light", 0, 0)
    before = jnp.cumsum(mine, axis=0) - mine
    back = lax.all_to_all(before, "light", 0, 0)
    return back.transpose(1, 0, 2).reshape(cells, columns)


def shade_kernel(facing_ref, dens_ref, emit_ref, out_ref, part_ref, *, light_scale, view_scale):
    rows, cells, _ = dens_ref.shape
    blocks, width = out_ref.shape[0], out_ref.shape[-1]

    def row(l, depth):
        dens = dens_ref[l]
        emit = emit_ref[l]
        tau_light = dens * light_scale
        step = jnp.exp(-(dens * view_scale))
        base = emit * (1.0 - step)
        shaded = base * jnp.exp(-depth)
        s = [step[v:v + 1] for v in range(cells)]
        flip = facing_ref[l] == 1
        ahead = [None] * cells
        behind = [None] * cells
        ahead[0] = jnp.ones_like(s[0])
        for v in range(1, cells):
            ahead[v] = ahead[v - 1] * s[v - 1]
        behind[cells - 1] = jnp.ones_like(s[0])
        for v in range(cells - 2, -1, -1):
            behind[v] = behind[v + 1] * s[v + 1]
        weight = [jnp.where(flip, behind[v], ahead[v]) for v in range(cells)]
        flat = weight[0] * base[0:1]
        for v in range(1, cells):
            flat = flat + weight[v] * base[v:v + 1]
        trans = ahead[cells - 1] * s[cells - 1]
        for b in range(blocks):
            cut = slice(b * width, (b + 1) * width)
            out_ref[b, 0, 0, pl.ds(l, 1), :] = 0.2 * flat[:, cut]
            out_ref[b, 1, 0, pl.ds(l, 1), :] = trans[:, cut]
            for v in range(cells):
                part_ref[v, b, 0, pl.ds(l, 1), :] = (weight[v] * shaded[v:v + 1])[:, cut]
        return depth + tau_light

    lax.fori_loop(0, rows, row, jnp.zeros(dens_ref.shape[1:], jnp.float32), unroll=8)


def shade(facing, density, emission, light_scale, view_scale, blocks, width):
    rows, cells, columns = density.shape
    tile = blocks * width
    tiles = columns // tile
    body = lambda *refs: shade_kernel(*refs, light_scale=light_scale, view_scale=view_scale)
    return pl.pallas_call(
        body,
        grid=(tiles,),
        in_specs=[
            pl.BlockSpec(memory_space=pltpu.SMEM),
            pl.BlockSpec((rows, cells, tile), lambda j: (0, 0, j)),
            pl.BlockSpec((rows, cells, tile), lambda j: (0, 0, j)),
        ],
        out_specs=[
            pl.BlockSpec((blocks, 2, 1, rows, width), lambda j: (0, 0, j, 0, 0)),
            pl.BlockSpec((cells, blocks, 1, rows, width), lambda j: (0, 0, j, 0, 0)),
        ],
        out_shape=[
            jax.ShapeDtypeStruct((blocks, 2, tiles, rows, width), jnp.float32),
            jax.ShapeDtypeStruct((cells, blocks, tiles, rows, width), jnp.float32),
        ],
        cost_estimate=pl.CostEstimate(
            flops=40 * density.size, transcendentals=2 * density.size, bytes_accessed=4 * 4 * density.size + 8 * rows * columns
        ),
    )(facing, density, emission)


def composite(colors, transes, reversed_rows):
    count = colors.shape[0]
    forward = colors[count - 1]
    for j in range(count - 2, -1, -1):
        forward = colors[j] + transes[j] * forward
    backward = colors[0]
    for j in range(1, count):
        backward = colors[j] + transes[j] * backward
    return jnp.where(reversed_rows, backward, forward)


def shards(density, emission, facing):
    rows, cells, columns = density.shape
    light_count = lax.axis_size("light")
    z_count = lax.axis_size("vz")
    x_count = lax.axis_size("vx")
    view_count = z_count * x_count
    tau_light = density * (1.0 / (rows * light_count))
    slab_depth = jnp.sum(tau_light, axis=0)
    reversed_rows = facing == 1
    width = columns // view_count
    unshaded, parts = shade(
        facing, density, emission, 1.0 / (rows * light_count), 1.0 / (cells * view_count), x_count, width
    )
    incoming = light_prefix(slab_depth)
    light = jnp.exp(-incoming).reshape(cells, z_count, x_count, 1, width).transpose(0, 2, 1, 3, 4)
    color = unshaded[:, 0] + jnp.sum(light * parts, axis=0)
    stacked = jnp.stack([color, unshaded[:, 1]], axis=1)
    along_x = lax.all_to_all(stacked, "vx", 0, 0)
    color_x = composite(along_x[:, 0], along_x[:, 1], reversed_rows[None, :, None])
    trans_x = jnp.prod(along_x[:, 1], axis=0)
    along_z = lax.all_to_all(jnp.stack([color_x, trans_x], axis=1), "vz", 0, 0)
    radiance = composite(along_z[:, 0], along_z[:, 1], reversed_rows[:, None])
    coverage = jnp.prod(along_z[:, 1], axis=0)
    return (radiance, coverage)


def view_split(mesh):
    row = mesh.devices.reshape(mesh.devices.shape[0], -1)[0]
    coords = [getattr(d, "coords", None) for d in row]
    if any(c is None for c in coords):
        return 1
    first_z = coords[0][2]
    x_extent = sum(1 for c in coords if c[2] == first_z)
    return 4 * x_extent if len(row) % (4 * x_extent) == 0 else x_extent


def solution(mesh):
    x_count = view_split(mesh)
    light_count, view_count = mesh.devices.shape
    split = Mesh(mesh.devices.reshape(light_count, view_count // x_count, x_count), ("light",) + VIEW)
    return jax.shard_map(
        shards,
        mesh=split,
        in_specs=(P("light", VIEW, None), P("light", VIEW, None), P("light")),
        out_specs=(P("light", VIEW), P("light", VIEW)),
        check_vma=False,
    )
```
